32 devices in a mesh: ri: 8 (over z, core), ao: 4 (over y, x).
Axes of the slice: x: 2, y: 2, z: 4, core: 2. Of those that a mesh axis runs over, the one named last changes fastest.
Arguments:
- three_center: bfloat16 [128, 512, 512], P('ri', 'ao'), as said below
- slab_tensor: bfloat16 [16, 512, 512], P('ri', 'ao'), as said below
- occ_green: bfloat16 [512, 512], P('ao'), as said below
- virt_green: bfloat16 [512, 512], P('ao'), as said below
- pattern: int32 [32, 32], replicated, may hold values from 0 to 1, as said below
- atom_sizes: int32 [32], replicated, may hold values from 6 to 16, as said below
Outputs:
- polar_slab: float32 [128, 16], P('ri')
The draws below stay inside these ranges and needn't reach their ends.
Inputs may be any that keep to these rules, and one draw needn't show every extreme that they name: three_center is symmetric in its last two dimensions. slab_tensor is symmetric in its last two dimensions. `occ_green`: symmetric matrix. `virt_green`: symmetric matrix. `pattern`: symmetric 0/1 matrix with ones on the diagonal. `atom_sizes`: some atom block has all 16 functions live.
All inputs are finite; a program needn't handle non-finite values.
Results may differ from the reference program's by a relative error of at most 0.0041.
Values may be sent and summed in bfloat16 or wider, within the bound.
No kernel may reach another device: no remote copies, remote signals or barrier semaphores. Data moves between devices by JAX's collectives and lax.ppermute only.
A program may use at most 128 MiB of HBM per device.

```python
import jax
import jax.numpy as jnp
from jax import lax

ATOM_BS = 16
RI_DEV = 16
NAO = 512
RI = 128
SLAB = 16
NATOMS = 32
N_RI = 8


def symmetric_normal(rng_key, order):
    normals = jax.random.normal(rng_key, (order, order), jnp.float32)
    return (normals + normals.T) * 0.70710678


def tensor_rows(rng_key, row_total):

    def one_row(row_number):
        return symmetric_normal(jax.random.fold_in(rng_key, row_number), NAO).astype(jnp.bfloat16)
    return lax.map(one_row, jnp.arange(row_total, dtype=jnp.int32))


def draw_three_center(rng_key, part_index):
    return tensor_rows(jax.random.fold_in(rng_key, 11), RI)


def draw_slab_tensor(rng_key, part_index):
    return tensor_rows(jax.random.fold_in(rng_key, 12), SLAB)


def draw_occ_green(rng_key, part_index):
    values = symmetric_normal(jax.random.fold_in(rng_key, 13), NAO) / jnp.sqrt(jnp.float32(NAO))
    return values.astype(jnp.bfloat16)


def draw_virt_green(rng_key, part_index):
    values = symmetric_normal(jax.random.fold_in(rng_key, 14), NAO) / jnp.sqrt(jnp.float32(NAO))
    return values.astype(jnp.bfloat16)


def draw_pattern(rng_key, part_index):
    coin_flips = jax.random.randint(jax.random.fold_in(rng_key, 15), (NATOMS, NATOMS), 0, 2, jnp.int32)
    upper_half = jnp.triu(coin_flips, 1)
    return upper_half + upper_half.T + jnp.eye(NATOMS, dtype=jnp.int32)


def draw_atom_sizes(rng_key, part_index):
    atom_counts = jax.random.randint(jax.random.fold_in(rng_key, 16), (NATOMS,), 6, ATOM_BS + 1, jnp.int32)
    forced_atom = jax.random.randint(jax.random.fold_in(rng_key, 17), (), 0, NATOMS, jnp.int32)
    return jnp.where(jnp.arange(NATOMS, dtype=jnp.int32) == forced_atom, ATOM_BS, atom_counts)


def setup_inputs(seed: int = 0) -> dict:
    splits = jax.random.split(jax.random.key(seed), 7)
    return {
        "three_center": draw_three_center(jax.random.fold_in(splits[6], 71), 0),
        "slab_tensor": draw_slab_tensor(jax.random.fold_in(splits[6], 71), 0),
        "occ_green": draw_occ_green(jax.random.fold_in(splits[6], 71), 0),
        "virt_green": draw_virt_green(jax.random.fold_in(splits[6], 71), 0),
        "pattern": draw_pattern(jax.random.fold_in(splits[6], 71), 0),
        "atom_sizes": draw_atom_sizes(jax.random.fold_in(splits[6], 71), 0),
    }


def live_functions(atom_sizes):
    atom_count = atom_sizes.shape[0]
    per_slot = jnp.broadcast_to(atom_sizes[:, None], (atom_count, ATOM_BS)).reshape(-1)
    slot_ids = jnp.broadcast_to(jnp.arange(ATOM_BS, dtype=jnp.int32)[None, :], (atom_count, ATOM_BS)).reshape(-1)
    return (slot_ids < per_slot).astype(jnp.float32)


def expand_pattern(pattern_rows):
    row_atoms = pattern_rows.shape[0]
    col_atoms = pattern_rows.shape[1]
    grown = jnp.broadcast_to(pattern_rows[:, None, :, None], (row_atoms, ATOM_BS, col_atoms, ATOM_BS))
    return grown.reshape(row_atoms * ATOM_BS, col_atoms * ATOM_BS).astype(jnp.float32)


def reference(three_center, slab_tensor, occ_green, virt_green, pattern, atom_sizes):
    live_mask = live_functions(atom_sizes)
    screen = (expand_pattern(pattern) * live_mask[:, None] * live_mask[None, :]).astype(jnp.bfloat16)

    def slab_weight(one_slab):
        masked_slab = one_slab * screen
        left_product = jnp.dot(occ_green, masked_slab, preferred_element_type=jnp.float32).astype(jnp.bfloat16)
        return jnp.dot(left_product, virt_green.T, preferred_element_type=jnp.float32).astype(jnp.bfloat16)

    weighted = lax.map(slab_weight, slab_tensor)
    weight_flat = weighted.reshape(SLAB, NAO * NAO)
    blocks = three_center.reshape(N_RI, RI_DEV, NAO, NAO)

    def block_polar(block_in):
        masked_block = (block_in * screen[None]).reshape(RI_DEV, NAO * NAO)
        return jnp.dot(masked_block, weight_flat.T, preferred_element_type=jnp.float32)

    polar = lax.map(block_polar, blocks).reshape(RI, SLAB)
    return polar / NAO
```

```python
import jax
import jax.numpy as jnp
from jax import lax
from jax.experimental import pallas as pl
from jax.experimental.pallas import tpu as pltpu
from jax.sharding import PartitionSpec as P

ATOM_BS = 16
TILE = 16


def top_bit(k):
    return k.bit_length() - 1


def which(a, k):
    return lax.shift_right_logical(a, jnp.int32(top_bit(k))) & 1


def tri_masks(block):
    row = lax.broadcasted_iota(jnp.int32, (block, block), 0)
    col = lax.broadcasted_iota(jnp.int32, (block, block), 1)
    return row > col, row == col


def fold_diagonal(first, second, below, on):
    folded = jnp.where(below | on, first, second)
    diagonal = jnp.sum(jnp.where(on, second, 0.0), axis=0, keepdims=True)
    return folded, diagonal


def block_at(ref, index, block):
    return ref[:, pl.ds(pl.multiple_of(index * block, block), block)]


def prep_kernel(sizes_ref, pattern_ref, slab_ref, occ_ref, virt_ref, pay_ref, screen_ref, mask_ref):
    block = occ_ref.shape[0]
    total = occ_ref.shape[1]
    ao = total // block
    atoms = pattern_ref.shape[0]
    f32, bf16 = jnp.float32, jnp.bfloat16
    a = lax.axis_index("ao")
    row_atom = lax.shift_right_logical(
        lax.broadcasted_iota(jnp.int32, (block, atoms), 0), jnp.int32(4)
    ) + a * (block // ATOM_BS)
    pick_row = row_atom == lax.broadcasted_iota(jnp.int32, (block, atoms), 1)
    col_atom = lax.shift_right_logical(
        lax.broadcasted_iota(jnp.int32, (atoms, total), 1), jnp.int32(4)
    )
    pick_col = (col_atom == lax.broadcasted_iota(jnp.int32, (atoms, total), 0)).astype(f32).astype(bf16)
    sizes = sizes_ref[...].astype(f32)
    size_row = jnp.sum(jnp.where(pick_row, jnp.broadcast_to(sizes, (block, atoms)), 0.0), axis=1, keepdims=True)
    size_col = jnp.dot(
        jnp.broadcast_to(sizes, (8, atoms)).astype(bf16), pick_col, preferred_element_type=f32
    )[0:1]
    rows = jnp.dot(
        pick_row.astype(f32).astype(bf16), pattern_ref[...].astype(f32).astype(bf16),
        preferred_element_type=f32,
    ).astype(bf16)
    kept = jnp.dot(rows, pick_col, preferred_element_type=f32)
    slot_row = (lax.broadcasted_iota(jnp.int32, (block, total), 0) & (ATOM_BS - 1)).astype(f32)
    slot_col = (lax.broadcasted_iota(jnp.int32, (block, total), 1) & (ATOM_BS - 1)).astype(f32)
    live = (slot_row < size_row) & (slot_col < size_col)
    mask_ref[...] = jnp.where(live, kept, 0.0).astype(bf16)
    below, on = tri_masks(block)
    half = ao * block + TILE
    for k in range(1, ao):
        screen = block_at(mask_ref, a ^ k, block)
        screen_ref[:, k * block : (k + 1) * block] = screen
        matrix = which(a, k)
        start = (k - 1) * block
        cols = pl.ds(pl.multiple_of((a ^ k) * block, block), block)
        pay_ref[start : start + block, :] = slab_ref[matrix, :, cols] * screen
        pay_ref[half + start : half + start + block, :] = jnp.where(
            matrix == 0, occ_ref[:, cols], virt_ref[:, cols]
        )
    screen = block_at(mask_ref, a, block)
    screen_ref[:, 0:block] = screen
    own = pl.ds(pl.multiple_of(a * block, block), block)
    start = (ao - 1) * block
    pairs = (
        (start, (slab_ref[0, :, own] * screen).astype(f32), (slab_ref[1, :, own] * screen).astype(f32)),
        (half + start, occ_ref[:, own].astype(f32), virt_ref[:, own].astype(f32)),
    )
    for at, first, second in pairs:
        folded, diagonal = fold_diagonal(first, second, below, on)
        pay_ref[at : at + block, :] = folded.astype(bf16)
        pay_ref[at + block : at + block + TILE, :] = jnp.broadcast_to(diagonal, (TILE, block)).astype(bf16)


def unfold(pays, base, a, ao, block, put):
    below, on = tri_masks(block)
    for m in range(ao):
        for j in range(m + 1, ao):
            k = m ^ j
            at = base + (k - 1) * block
            here = pays[m][at : at + block, :]
            there = pays[j][at : at + block, :]
            here_t = here.T
            there_t = there.T
            lower = which(a ^ m, k) == 0
            put(0, m, j, jnp.where(lower, here, there_t))
            put(0, j, m, jnp.where(lower, here_t, there))
            put(1, m, j, jnp.where(lower, there_t, here))
            put(1, j, m, jnp.where(lower, there, here_t))
        at = base + (ao - 1) * block
        folded = pays[m][at : at + block, :].astype(jnp.float32)
        folded_t = folded.T
        diagonal = pays[m][at + block : at + block + TILE, :].astype(jnp.float32)[0:1]
        put(0, m, m, jnp.where(below | on, folded, folded_t).astype(jnp.bfloat16))
        put(
            1, m, m,
            jnp.where(below, folded_t, jnp.where(on, jnp.broadcast_to(diagonal, (block, block)), folded)).astype(
                jnp.bfloat16
            ),
        )


def transform_kernel(ao, block, *refs):
    pays = refs[:ao]
    screen_ref, out_ref, slab_ref, green_ref, left_ref = refs[ao:]
    total = ao * block
    a = lax.axis_index("ao")
    half = total + TILE
    f32, bf16 = jnp.float32, jnp.bfloat16

    def put_slab(matrix, row, col, value):
        slab_ref[matrix, row * block : (row + 1) * block, col * block : (col + 1) * block] = value

    def put_green(matrix, row, col, value):
        at = (total if matrix == 0 else 0) + col * block
        green_ref[row, :, at : at + block] = value

    unfold(pays, half, a, ao, block, put_green)
    unfold(pays, 0, a, ao, block, put_slab)
    both = jnp.concatenate([green_ref[0, :, total:], green_ref[0, :, :total]], axis=0)
    for q in range(2):
        left = jnp.dot(both, slab_ref[q], preferred_element_type=f32).astype(bf16)
        left_ref[q, :, :total] = left[:block]
        left_ref[q, :, total:] = left[block:]
    last = (((1,), (1,)), ((), ()))
    for k in range(1, ao):
        sums = lax.dot_general(left_ref[which(a, k)], green_ref[k], last, preferred_element_type=f32)
        screen = screen_ref[:, k * block : (k + 1) * block].astype(f32)
        out_ref[(k - 1) * block : k * block, :] = (sums * screen).astype(bf16)
    below, on = tri_masks(block)
    weight = jnp.where(on, 0.5, 1.0) * screen_ref[:, 0:block].astype(f32)
    first, second = (
        lax.dot_general(left_ref[q], green_ref[0], last, preferred_element_type=f32) * weight for q in range(2)
    )
    folded, diagonal = fold_diagonal(first, second, below, on)
    at = (ao - 1) * block
    out_ref[at : at + block, :] = folded.astype(bf16)
    out_ref[at + block : at + block + TILE, :] = jnp.broadcast_to(diagonal, (TILE, block)).astype(bf16)


def contract_kernel(count, ao, block, *refs):
    pays = refs[:count]
    tensor_ref, out_ref = refs[count:]
    ri_rows = tensor_ref.shape[0]
    a = lax.axis_index("ao")
    r = lax.axis_index("ri")
    f32, bf16 = jnp.float32, jnp.bfloat16
    groups = block // TILE
    last = (((1,), (1,)), ((), ()))

    def spread(values, rows_of):
        return jnp.concatenate(
            [
                jnp.concatenate([rows_of(v, slice(g * TILE, (g + 1) * TILE)) for v in values], axis=0)
                for g in range(groups)
            ],
            axis=1,
        )

    def tensor_block(k):
        cols = pl.ds(pl.multiple_of((a ^ k) * block, block), block)
        return spread(range(ri_rows), lambda p, rows: tensor_ref[p, rows, cols])

    below, on = tri_masks(block)
    at = (ao - 1) * block
    firsts, seconds = [], []
    for pay in pays:
        folded = pay[at : at + block, :].astype(f32)
        diagonal = pay[at + block : at + block + TILE, :].astype(f32)[0:1]
        firsts.append(jnp.where(below | on, folded, 0.0).astype(bf16))
        seconds.append(
            jnp.where(below, 0.0, jnp.where(on, jnp.broadcast_to(diagonal, (block, block)), folded)).astype(bf16)
        )
    sums = lax.dot_general(
        spread(firsts + seconds, lambda v, rows: v[rows]), tensor_block(0), last, preferred_element_type=f32
    )
    half = count * TILE
    sums = [sums[:half], sums[half:]]
    for k in range(1, ao):
        start = (k - 1) * block
        part = lax.dot_general(
            spread(pays, lambda pay, rows: pay[start + rows.start : start + rows.stop, :]),
            tensor_block(k),
            last,
            preferred_element_type=f32,
        )
        to_first = which(a, k) == 0
        sums[0] = sums[0] + jnp.where(to_first, part, 0.0)
        sums[1] = sums[1] + jnp.where(to_first, 0.0, part)
    width = ri_rows * TILE
    row = lax.broadcasted_iota(jnp.int32, (half, width), 0)
    col = lax.broadcasted_iota(jnp.int32, (half, width), 1)
    same = (row & (TILE - 1)) == (col & (TILE - 1))
    traces = jnp.concatenate(
        [jnp.where(same, s, 0.0).reshape(count, TILE, width).sum(axis=1) for s in sums], axis=0
    )
    pick = (
        lax.shift_right_logical(lax.broadcasted_iota(jnp.int32, (ri_rows, width), 1), jnp.int32(4))
        == lax.broadcasted_iota(jnp.int32, (ri_rows, width), 0)
    ).astype(f32)
    by_source = lax.dot_general(
        pick, traces, last, precision=lax.Precision.HIGHEST, preferred_element_type=f32
    )
    source = lax.broadcasted_iota(jnp.int32, (2 * count, 2 * count), 0)
    target = lax.broadcasted_iota(jnp.int32, (2 * count, 2 * count), 1)
    place = ((jnp.where(source < count, source, source - count) ^ r) * 2 + (source >= count).astype(jnp.int32)) == target
    ordered = jnp.dot(
        by_source, place.astype(f32), precision=lax.Precision.HIGHEST, preferred_element_type=f32
    )
    out_ref[...] = ordered * (1.0 / (ao * block))


def exchange(value, axis, size, k):
    return lax.ppermute(value, axis, [(i, i ^ k) for i in range(size)])


def shards(ri, ao, three_center, slab_tensor, occ_green, virt_green, pattern, atom_sizes):
    block = occ_green.shape[0]
    total = occ_green.shape[1]
    ri_rows = three_center.shape[0]
    atoms = pattern.shape[0]
    half = total + TILE
    bf16 = jnp.bfloat16
    vmem = pl.BlockSpec(memory_space=pltpu.VMEM)
    pay, screen = pl.pallas_call(
        prep_kernel,
        out_shape=(
            jax.ShapeDtypeStruct((2 * half, block), bf16),
            jax.ShapeDtypeStruct((block, total), bf16),
        ),
        in_specs=[vmem] * 5,
        out_specs=(vmem, vmem),
        scratch_shapes=[pltpu.VMEM((block, total), bf16)],
        name="prep",
    )(atom_sizes.reshape(1, atoms), pattern, slab_tensor, occ_green, virt_green)
    pays = [pay] + [exchange(pay, "ao", ao, k) for k in range(1, ao)]
    weighted = pl.pallas_call(
        lambda *refs: transform_kernel(ao, block, *refs),
        out_shape=jax.ShapeDtypeStruct((half, block), bf16),
        in_specs=[vmem] * (ao + 1),
        out_specs=vmem,
        scratch_shapes=[
            pltpu.VMEM((2, total, total), bf16),
            pltpu.VMEM((ao, block, 2 * total), bf16),
            pltpu.VMEM((2, block, 2 * total), bf16),
        ],
        name="transform",
    )(*pays, screen)
    sources = [weighted]
    for k in range(2, ri, 2):
        sources.append(exchange(weighted, "ri", ri, k))
    arrived = []
    for value in sources:
        arrived.append(value)
        arrived.append(exchange(value, "ri", ri, 1))
    part = pl.pallas_call(
        lambda *refs: contract_kernel(ri, ao, block, *refs),
        out_shape=jax.ShapeDtypeStruct((ri_rows, 2 * ri), jnp.float32),
        in_specs=[vmem] * (ri + 1),
        out_specs=vmem,
        name="contract",
    )(*arrived, three_center)
    parts = [part] + [exchange(part, "ao", ao, k) for k in range(1, ao)]
    while len(parts) > 1:
        parts = [parts[i] + parts[i + 1] for i in range(0, len(parts), 2)]
    return parts[0]


def solution(mesh):
    placed = (P("ri", "ao", None), P("ri", "ao", None), P("ao", None), P("ao", None), P(), P())
    ri, ao = mesh.shape["ri"], mesh.shape["ao"]

    def body(*args):
        return shards(ri, ao, *args)

    return jax.shard_map(body, mesh=mesh, in_specs=placed, out_specs=P("ri", None), check_vma=False)
```

```python
import math

import jax
import jax.numpy as jnp
from jax import lax
from jax.experimental import pallas as pl
from jax.experimental.pallas import tpu as pltpu
from jax.sharding import PartitionSpec as P

ATOM_BS = 16
TILE = 16


def top_bit(k):
    return k.bit_length() - 1


def which(a, k):
    return lax.shift_right_logical(a, jnp.int32(top_bit(k))) & 1


def tri_masks(block):
    row = lax.broadcasted_iota(jnp.int32, (block, block), 0)
    col = lax.broadcasted_iota(jnp.int32, (block, block), 1)
    return row > col, row == col


def fold_diagonal(first, second, below, on):
    folded = jnp.where(below | on, first, second)
    diagonal = jnp.sum(jnp.where(on, second, 0.0), axis=0, keepdims=True)
    return folded, diagonal


def block_at(ref, index, block):
    return ref[:, pl.ds(pl.multiple_of(index * block, block), block)]


def prep_kernel(*refs):
    hbm, (pay_ref, screen_ref), copied, mask_ref, sems = refs[:5], refs[5:7], refs[7:12], refs[12], refs[13]
    copies = [pltpu.make_async_copy(src, dst, sems.at[i]) for i, (src, dst) in enumerate(zip(hbm, copied))]
    for copy in copies:
        copy.start()
    sizes_ref, pattern_ref, slab_ref, occ_ref, virt_ref = copied
    block = occ_ref.shape[0]
    total = occ_ref.shape[1]
    ao = total // block
    atoms = pattern_ref.shape[0]
    f32, bf16 = jnp.float32, jnp.bfloat16
    a = lax.axis_index("ao")
    row_atom = lax.shift_right_logical(
        lax.broadcasted_iota(jnp.int32, (block, atoms), 0), jnp.int32(4)
    ) + a * (block // ATOM_BS)
    pick_row = row_atom == lax.broadcasted_iota(jnp.int32, (block, atoms), 1)
    col_atom = lax.shift_right_logical(
        lax.broadcasted_iota(jnp.int32, (atoms, total), 1), jnp.int32(4)
    )
    pick_col = (col_atom == lax.broadcasted_iota(jnp.int32, (atoms, total), 0)).astype(f32).astype(bf16)
    copies[0].wait()
    copies[1].wait()
    sizes = sizes_ref[...].astype(f32)
    size_row = jnp.sum(jnp.where(pick_row, jnp.broadcast_to(sizes, (block, atoms)), 0.0), axis=1, keepdims=True)
    size_col = jnp.dot(
        jnp.broadcast_to(sizes, (8, atoms)).astype(bf16), pick_col, preferred_element_type=f32
    )[0:1]
    rows = jnp.dot(
        pick_row.astype(f32).astype(bf16), pattern_ref[...].astype(f32).astype(bf16),
        preferred_element_type=f32,
    ).astype(bf16)
    kept = jnp.dot(rows, pick_col, preferred_element_type=f32)
    slot_row = (lax.broadcasted_iota(jnp.int32, (block, total), 0) & (ATOM_BS - 1)).astype(f32)
    slot_col = (lax.broadcasted_iota(jnp.int32, (block, total), 1) & (ATOM_BS - 1)).astype(f32)
    live = (slot_row < size_row) & (slot_col < size_col)
    mask_ref[...] = jnp.where(live, kept, 0.0).astype(bf16)
    below, on = tri_masks(block)
    half = ao * block + TILE
    for copy in copies[2:]:
        copy.wait()
    for k in range(1, ao):
        screen = block_at(mask_ref, a ^ k, block)
        screen_ref[:, k * block : (k + 1) * block] = screen
        matrix = which(a, k)
        start = (k - 1) * block
        cols = pl.ds(pl.multiple_of((a ^ k) * block, block), block)
        pay_ref[start : start + block, :] = slab_ref[matrix, :, cols] * screen
        pay_ref[half + start : half + start + block, :] = jnp.where(
            matrix == 0, occ_ref[:, cols], virt_ref[:, cols]
        )
    screen = block_at(mask_ref, a, block)
    screen_ref[:, 0:block] = screen
    own = pl.ds(pl.multiple_of(a * block, block), block)
    start = (ao - 1) * block
    pairs = (
        (start, (slab_ref[0, :, own] * screen).astype(f32), (slab_ref[1, :, own] * screen).astype(f32)),
        (half + start, occ_ref[:, own].astype(f32), virt_ref[:, own].astype(f32)),
    )
    for at, first, second in pairs:
        folded, diagonal = fold_diagonal(first, second, below, on)
        pay_ref[at : at + block, :] = folded.astype(bf16)
        pay_ref[at + block : at + block + TILE, :] = jnp.broadcast_to(diagonal, (TILE, block)).astype(bf16)


def unfold(pays, base, a, ao, block, put):
    below, on = tri_masks(block)
    for m in range(ao):
        for j in range(m + 1, ao):
            k = m ^ j
            at = base + (k - 1) * block
            here = pays[m][at : at + block, :]
            there = pays[j][at : at + block, :]
            here_t = here.T
            there_t = there.T
            lower = which(a ^ m, k) == 0
            put(0, m, j, jnp.where(lower, here, there_t))
            put(0, j, m, jnp.where(lower, here_t, there))
            put(1, m, j, jnp.where(lower, there_t, here))
            put(1, j, m, jnp.where(lower, there, here_t))
        at = base + (ao - 1) * block
        folded = pays[m][at : at + block, :].astype(jnp.float32)
        folded_t = folded.T
        diagonal = pays[m][at + block : at + block + TILE, :].astype(jnp.float32)[0:1]
        put(0, m, m, jnp.where(below | on, folded, folded_t).astype(jnp.bfloat16))
        put(
            1, m, m,
            jnp.where(below, folded_t, jnp.where(on, jnp.broadcast_to(diagonal, (block, block)), folded)).astype(
                jnp.bfloat16
            ),
        )


def transform_kernel(ao, block, *refs):
    pays = refs[:ao]
    screen_ref, _, out_ref, slab_ref, green_ref, left_ref = refs[ao:]
    total = ao * block
    a = lax.axis_index("ao")
    half = total + TILE
    f32, bf16 = jnp.float32, jnp.bfloat16

    def put_slab(matrix, row, col, value):
        slab_ref[matrix, row * block : (row + 1) * block, col * block : (col + 1) * block] = value

    def put_green(matrix, row, col, value):
        at = (total if matrix == 0 else 0) + col * block
        green_ref[row, :, at : at + block] = value

    unfold(pays, half, a, ao, block, put_green)
    unfold(pays, 0, a, ao, block, put_slab)
    both = jnp.concatenate([green_ref[0, :, total:], green_ref[0, :, :total]], axis=0)
    for q in range(2):
        left = jnp.dot(both, slab_ref[q], preferred_element_type=f32).astype(bf16)
        left_ref[q, :, :total] = left[:block]
        left_ref[q, :, total:] = left[block:]
    last = (((1,), (1,)), ((), ()))
    for k in range(1, ao):
        sums = lax.dot_general(left_ref[which(a, k)], green_ref[k], last, preferred_element_type=f32)
        screen = screen_ref[:, k * block : (k + 1) * block].astype(f32)
        out_ref[(k - 1) * block : k * block, :] = (sums * screen).astype(bf16)
    below, on = tri_masks(block)
    weight = jnp.where(on, 0.5, 1.0) * screen_ref[:, 0:block].astype(f32)
    first, second = (
        lax.dot_general(left_ref[q], green_ref[0], last, preferred_element_type=f32) * weight for q in range(2)
    )
    folded, diagonal = fold_diagonal(first, second, below, on)
    at = (ao - 1) * block
    out_ref[at : at + block, :] = folded.astype(bf16)
    out_ref[at + block : at + block + TILE, :] = jnp.broadcast_to(diagonal, (TILE, block)).astype(bf16)


def stage_kernel(tensor_hbm, _, out_ref, tensor_ref, sem):
    ri_rows, block, _ = tensor_ref.shape
    a = lax.axis_index("ao")
    copy = pltpu.make_async_copy(tensor_hbm, tensor_ref, sem)
    copy.start()
    copy.wait()
    for k in range(out_ref.shape[0]):
        cols = pl.ds(pl.multiple_of((a ^ k) * block, block), block)
        for g in range(block // TILE):
            for p in range(ri_rows):
                out_ref[k, p * TILE : (p + 1) * TILE, g * block : (g + 1) * block] = tensor_ref[
                    p, g * TILE : (g + 1) * TILE, cols
                ]


def contract_kernel(count, ao, block, *refs):
    pays = refs[:count]
    tensor_ref, out_ref = refs[count:]
    ri_rows = tensor_ref.shape[1] // TILE
    a = lax.axis_index("ao")
    r = lax.axis_index("ri")
    f32, bf16 = jnp.float32, jnp.bfloat16
    groups = block // TILE
    last = (((1,), (1,)), ((), ()))

    def spread(values, rows_of):
        return jnp.concatenate(
            [
                jnp.concatenate([rows_of(v, slice(g * TILE, (g + 1) * TILE)) for v in values], axis=0)
                for g in range(groups)
            ],
            axis=1,
        )

    below, on = tri_masks(block)
    at = (ao - 1) * block
    firsts, seconds = [], []
    for pay in pays:
        folded = pay[at : at + block, :].astype(f32)
        diagonal = pay[at + block : at + block + TILE, :].astype(f32)[0:1]
        firsts.append(jnp.where(below | on, folded, 0.0).astype(bf16))
        seconds.append(
            jnp.where(below, 0.0, jnp.where(on, jnp.broadcast_to(diagonal, (block, block)), folded)).astype(bf16)
        )
    sums = lax.dot_general(
        spread(firsts + seconds, lambda v, rows: v[rows]), tensor_ref[0], last, preferred_element_type=f32
    )
    half = count * TILE
    sums = [sums[:half], sums[half:]]
    for k in range(1, ao):
        start = (k - 1) * block
        part = lax.dot_general(
            spread(pays, lambda pay, rows: pay[start + rows.start : start + rows.stop, :]),
            tensor_ref[k],
            last,
            preferred_element_type=f32,
        )
        to_first = which(a, k) == 0
        sums[0] = sums[0] + jnp.where(to_first, part, 0.0)
        sums[1] = sums[1] + jnp.where(to_first, 0.0, part)
    width = ri_rows * TILE
    row = lax.broadcasted_iota(jnp.int32, (half, width), 0)
    col = lax.broadcasted_iota(jnp.int32, (half, width), 1)
    same = (row & (TILE - 1)) == (col & (TILE - 1))
    traces = jnp.concatenate(
        [jnp.where(same, s, 0.0).reshape(count, TILE, width).sum(axis=1) for s in sums], axis=0
    )
    pick = (
        lax.shift_right_logical(lax.broadcasted_iota(jnp.int32, (ri_rows, width), 1), jnp.int32(4))
        == lax.broadcasted_iota(jnp.int32, (ri_rows, width), 0)
    ).astype(f32)
    by_source = lax.dot_general(
        pick, traces, last, precision=lax.Precision.HIGHEST, preferred_element_type=f32
    )
    source = lax.broadcasted_iota(jnp.int32, (2 * count, 2 * count), 0)
    target = lax.broadcasted_iota(jnp.int32, (2 * count, 2 * count), 1)
    place = ((jnp.where(source < count, source, source - count) ^ r) * 2 + (source >= count).astype(jnp.int32)) == target
    ordered = jnp.dot(
        by_source, place.astype(f32), precision=lax.Precision.HIGHEST, preferred_element_type=f32
    )
    out_ref[...] = ordered * (1.0 / (ao * block))


def room(*arrays):
    total = sum(2 * math.prod(shape) for shape in arrays)
    return pltpu.CompilerParams(vmem_limit_bytes=min(2 * total + (4 << 20), 60 << 20))


def exchange(value, axis, size, k):
    return lax.ppermute(value, axis, [(i, i ^ k) for i in range(size)])


def shards(ri, ao, three_center, slab_tensor, occ_green, virt_green, pattern, atom_sizes):
    block = occ_green.shape[0]
    total = occ_green.shape[1]
    ri_rows = three_center.shape[0]
    atoms = pattern.shape[0]
    half = total + TILE
    bf16 = jnp.bfloat16
    vmem = pl.BlockSpec(memory_space=pltpu.VMEM)
    inputs = tuple(
        pltpu.with_memory_space_constraint(x, pltpu.HBM)
        for x in (atom_sizes.reshape(1, atoms), pattern, slab_tensor, occ_green, virt_green)
    )
    pay, screen = pl.pallas_call(
        prep_kernel,
        out_shape=(
            jax.ShapeDtypeStruct((2 * half, block), bf16),
            jax.ShapeDtypeStruct((block, total), bf16),
        ),
        in_specs=[pl.BlockSpec(memory_space=pltpu.HBM)] * 5,
        out_specs=(vmem, vmem),
        scratch_shapes=[pltpu.VMEM(x.shape, x.dtype) for x in inputs]
        + [pltpu.VMEM((block, total), bf16), pltpu.SemaphoreType.DMA((5,))],
        compiler_params=room((4 * half, block), (3 * block, total), (2 * block, 2 * total)),
        name="prep",
    )(*inputs)
    pays = [pay] + [exchange(pay, "ao", ao, k) for k in range(1, ao)]
    groups = block // TILE
    staged = pl.pallas_call(
        stage_kernel,
        out_shape=jax.ShapeDtypeStruct((ao, ri_rows * TILE, groups * block), bf16),
        in_specs=[pl.BlockSpec(memory_space=pltpu.HBM)] * 2,
        out_specs=vmem,
        scratch_shapes=[pltpu.VMEM(three_center.shape, bf16), pltpu.SemaphoreType.DMA],
        compiler_params=room((2 * ri_rows, block, total)),
        cost_estimate=pl.CostEstimate(flops=0, transcendentals=0, bytes_accessed=8 * ri_rows * block * total),
        name="stage",
    )(pltpu.with_memory_space_constraint(three_center, pltpu.HBM), pay)
    weighted = pl.pallas_call(
        lambda *refs: transform_kernel(ao, block, *refs),
        out_shape=jax.ShapeDtypeStruct((half, block), bf16),
        in_specs=[vmem] * (ao + 1) + [pl.BlockSpec(memory_space=pl.ANY)],
        out_specs=vmem,
        scratch_shapes=[
            pltpu.VMEM((2, total, total), bf16),
            pltpu.VMEM((ao, block, 2 * total), bf16),
            pltpu.VMEM((2, block, 2 * total), bf16),
        ],
        compiler_params=room((2 * half * ao, block), (2, total, total), (ao, block, 2 * total), (4, block, total)),
        name="transform",
    )(*pays, screen, staged)
    sources = [weighted]
    for k in range(2, ri, 2):
        sources.append(exchange(weighted, "ri", ri, k))
    arrived = []
    for value in sources:
        arrived.append(value)
        arrived.append(exchange(value, "ri", ri, 1))
    part = pl.pallas_call(
        lambda *refs: contract_kernel(ri, ao, block, *refs),
        out_shape=jax.ShapeDtypeStruct((ri_rows, 2 * ri), jnp.float32),
        in_specs=[vmem] * (ri + 1),
        out_specs=vmem,
        compiler_params=room((half * ri, block), (2 * ri_rows, block, total)),
        name="contract",
    )(*arrived, staged)
    parts = [part] + [exchange(part, "ao", ao, k) for k in range(1, ao)]
    while len(parts) > 1:
        parts = [parts[i] + parts[i + 1] for i in range(0, len(parts), 2)]
    return parts[0]


def solution(mesh):
    placed = (P("ri", "ao", None), P("ri", "ao", None), P("ao", None), P("ao", None), P(), P())
    ri, ao = mesh.shape["ri"], mesh.shape["ao"]

    def body(*args):
        return shards(ri, ao, *args)

    return jax.shard_map(body, mesh=mesh, in_specs=placed, out_specs=P("ri", None), check_vma=False)
```

```python
import math

import jax
import jax.numpy as jnp
from jax import lax
from jax.experimental import pallas as pl
from jax.experimental.pallas import tpu as pltpu
from jax.sharding import PartitionSpec as P

ATOM_BS = 16
TILE = 16


def top_bit(k):
    return k.bit_length() - 1


def which(a, k):
    return lax.shift_right_logical(a, jnp.int32(top_bit(k))) & 1


def tri_masks(block):
    row = lax.broadcasted_iota(jnp.int32, (block, block), 0)
    col = lax.broadcasted_iota(jnp.int32, (block, block), 1)
    return row > col, row == col


def fold_diagonal(first, second, below, on):
    folded = jnp.where(below | on, first, second)
    diagonal = jnp.sum(jnp.where(on, second, 0.0), axis=0, keepdims=True)
    return folded, diagonal


def block_at(ref, index, block):
    return ref[:, pl.ds(pl.multiple_of(index * block, block), block)]


def prep_kernel(*refs):
    hbm, copied, mask_ref, sems = refs[:5], refs[9:14], refs[14], refs[15]
    pay_ref, green_ref, part_ref, screen_ref = refs[5:9]
    copies = [pltpu.make_async_copy(src, dst, sems.at[i]) for i, (src, dst) in enumerate(zip(hbm, copied))]
    for copy in copies:
        copy.start()
    sizes_ref, pattern_ref, slab_ref, occ_ref, virt_ref = copied
    block = occ_ref.shape[0]
    total = occ_ref.shape[1]
    ao = total // block
    atoms = pattern_ref.shape[0]
    f32, bf16 = jnp.float32, jnp.bfloat16
    a = lax.axis_index("ao")
    row_atom = lax.shift_right_logical(
        lax.broadcasted_iota(jnp.int32, (block, atoms), 0), jnp.int32(4)
    ) + a * (block // ATOM_BS)
    pick_row = row_atom == lax.broadcasted_iota(jnp.int32, (block, atoms), 1)
    col_atom = lax.shift_right_logical(
        lax.broadcasted_iota(jnp.int32, (atoms, total), 1), jnp.int32(4)
    )
    pick_col = (col_atom == lax.broadcasted_iota(jnp.int32, (atoms, total), 0)).astype(f32).astype(bf16)
    copies[0].wait()
    copies[1].wait()
    sizes = sizes_ref[...].astype(f32)
    size_row = jnp.sum(jnp.where(pick_row, jnp.broadcast_to(sizes, (block, atoms)), 0.0), axis=1, keepdims=True)
    size_col = jnp.dot(
        jnp.broadcast_to(sizes, (8, atoms)).astype(bf16), pick_col, preferred_element_type=f32
    )[0:1]
    rows = jnp.dot(
        pick_row.astype(f32).astype(bf16), pattern_ref[...].astype(f32).astype(bf16),
        preferred_element_type=f32,
    ).astype(bf16)
    kept = jnp.dot(rows, pick_col, preferred_element_type=f32)
    slot_row = (lax.broadcasted_iota(jnp.int32, (block, total), 0) & (ATOM_BS - 1)).astype(f32)
    slot_col = (lax.broadcasted_iota(jnp.int32, (block, total), 1) & (ATOM_BS - 1)).astype(f32)
    live = (slot_row < size_row) & (slot_col < size_col)
    mask_ref[...] = jnp.where(live, kept, 0.0).astype(bf16)
    below, on = tri_masks(block)
    for copy in copies[2:]:
        copy.wait()
    for k in range(1, ao):
        screen = block_at(mask_ref, a ^ k, block)
        screen_ref[:, k * block : (k + 1) * block] = screen
        matrix = which(a, k)
        start = (k - 1) * block
        cols = pl.ds(pl.multiple_of((a ^ k) * block, block), block)
        pay_ref[start : start + block, :] = slab_ref[matrix, :, cols] * screen
        green_ref[start : start + block, :] = jnp.where(
            matrix == 0, occ_ref[:, cols], virt_ref[:, cols]
        )
    screen = block_at(mask_ref, a, block)
    screen_ref[:, 0:block] = screen
    own = pl.ds(pl.multiple_of(a * block, block), block)
    start = (ao - 1) * block
    pairs = (
        (pay_ref, (slab_ref[0, :, own] * screen).astype(f32), (slab_ref[1, :, own] * screen).astype(f32)),
        (green_ref, occ_ref[:, own].astype(f32), virt_ref[:, own].astype(f32)),
    )
    for ref, first, second in pairs:
        folded, diagonal = fold_diagonal(first, second, below, on)
        ref[start : start + block, :] = folded.astype(bf16)
        ref[start + block :, :] = jnp.broadcast_to(diagonal, (TILE, block)).astype(bf16)
    core = lax.axis_index("ri") & 1
    rows = block // 2
    for k in range(ao):
        part_ref[k * rows : (k + 1) * rows, :] = green_ref[
            pl.ds(pl.multiple_of(k * block + core * rows, TILE), rows), :
        ]
    part_ref[ao * rows :, :] = green_ref[ao * block :, :]


def whole_reader(ref, block):
    return lambda k: ref[k * block : (k + 1) * block, :] if k >= 0 else ref[ref.shape[0] - TILE :, :]


def halves_reader(mine, other, core, block):
    rows = block // 2

    def read(k):
        if k < 0:
            return mine[mine.shape[0] - TILE :, :]
        here, there = mine[k * rows : (k + 1) * rows, :], other[k * rows : (k + 1) * rows, :]
        return jnp.concatenate([jnp.where(core == 0, here, there), jnp.where(core == 0, there, here)], axis=0)

    return read


def unfold(reads, a, ao, block, put):
    below, on = tri_masks(block)
    for m in range(ao):
        for j in range(m + 1, ao):
            k = m ^ j
            here = reads[m](k - 1)
            there = reads[j](k - 1)
            here_t = here.T
            there_t = there.T
            lower = which(a ^ m, k) == 0
            put(0, m, j, jnp.where(lower, here, there_t))
            put(0, j, m, jnp.where(lower, here_t, there))
            put(1, m, j, jnp.where(lower, there_t, here))
            put(1, j, m, jnp.where(lower, there, here_t))
        folded = reads[m](ao - 1).astype(jnp.float32)
        folded_t = folded.T
        diagonal = reads[m](-1).astype(jnp.float32)[0:1]
        put(0, m, m, jnp.where(below | on, folded, folded_t).astype(jnp.bfloat16))
        put(
            1, m, m,
            jnp.where(below, folded_t, jnp.where(on, jnp.broadcast_to(diagonal, (block, block)), folded)).astype(
                jnp.bfloat16
            ),
        )


def transform_kernel(ao, block, *refs):
    pays, own, mine, other = refs[:ao], refs[ao], refs[ao + 1 : 2 * ao], refs[2 * ao : 3 * ao - 1]
    screen_ref, _, out_ref, slab_ref, green_ref, left_ref = refs[3 * ao - 1 :]
    total = ao * block
    a = lax.axis_index("ao")
    core = lax.axis_index("ri") & 1
    f32, bf16 = jnp.float32, jnp.bfloat16
    greens = [whole_reader(own, block)] + [halves_reader(x, y, core, block) for x, y in zip(mine, other)]

    def put_slab(matrix, row, col, value):
        slab_ref[matrix, row * block : (row + 1) * block, col * block : (col + 1) * block] = value

    def put_green(matrix, row, col, value):
        at = (total if matrix == 0 else 0) + col * block
        green_ref[row, :, at : at + block] = value

    unfold(greens, a, ao, block, put_green)
    unfold([whole_reader(x, block) for x in pays], a, ao, block, put_slab)
    both = jnp.concatenate([green_ref[0, :, total:], green_ref[0, :, :total]], axis=0)
    for q in range(2):
        left = jnp.dot(both, slab_ref[q], preferred_element_type=f32).astype(bf16)
        left_ref[q, :, :total] = left[:block]
        left_ref[q, :, total:] = left[block:]
    last = (((1,), (1,)), ((), ()))
    for k in range(1, ao):
        sums = lax.dot_general(left_ref[which(a, k)], green_ref[k], last, preferred_element_type=f32)
        screen = screen_ref[:, k * block : (k + 1) * block].astype(f32)
        out_ref[(k - 1) * block : k * block, :] = (sums * screen).astype(bf16)
    below, on = tri_masks(block)
    weight = jnp.where(on, 0.5, 1.0) * screen_ref[:, 0:block].astype(f32)
    first, second = (
        lax.dot_general(left_ref[q], green_ref[0], last, preferred_element_type=f32) * weight for q in range(2)
    )
    folded, diagonal = fold_diagonal(first, second, below, on)
    at = (ao - 1) * block
    out_ref[at : at + block, :] = folded.astype(bf16)
    out_ref[at + block : at + block + TILE, :] = jnp.broadcast_to(diagonal, (TILE, block)).astype(bf16)


def stage_kernel(tensor_hbm, _, out_ref, tensor_ref, sem):
    ri_rows, block, _ = tensor_ref.shape
    a = lax.axis_index("ao")
    copy = pltpu.make_async_copy(tensor_hbm, tensor_ref, sem)
    copy.start()
    copy.wait()
    for k in range(out_ref.shape[0]):
        cols = pl.ds(pl.multiple_of((a ^ k) * block, block), block)
        for g in range(block // TILE):
            for p in range(ri_rows):
                out_ref[k, p * TILE : (p + 1) * TILE, g * block : (g + 1) * block] = tensor_ref[
                    p, g * TILE : (g + 1) * TILE, cols
                ]


def contract_kernel(count, ao, block, *refs):
    pays = refs[:count]
    tensor_ref, out_ref = refs[count:]
    ri_rows = tensor_ref.shape[1] // TILE
    a = lax.axis_index("ao")
    r = lax.axis_index("ri")
    f32, bf16 = jnp.float32, jnp.bfloat16
    groups = block // TILE
    last = (((1,), (1,)), ((), ()))

    def spread(values, rows_of):
        return jnp.concatenate(
            [
                jnp.concatenate([rows_of(v, slice(g * TILE, (g + 1) * TILE)) for v in values], axis=0)
                for g in range(groups)
            ],
            axis=1,
        )

    below, on = tri_masks(block)
    at = (ao - 1) * block
    firsts, seconds = [], []
    for pay in pays:
        folded = pay[at : at + block, :].astype(f32)
        diagonal = pay[at + block : at + block + TILE, :].astype(f32)[0:1]
        firsts.append(jnp.where(below | on, folded, 0.0).astype(bf16))
        seconds.append(
            jnp.where(below, 0.0, jnp.where(on, jnp.broadcast_to(diagonal, (block, block)), folded)).astype(bf16)
        )
    sums = lax.dot_general(
        spread(firsts + seconds, lambda v, rows: v[rows]), tensor_ref[0], last, preferred_element_type=f32
    )
    half = count * TILE
    sums = [sums[:half], sums[half:]]
    for k in range(1, ao):
        start = (k - 1) * block
        part = lax.dot_general(
            spread(pays, lambda pay, rows: pay[start + rows.start : start + rows.stop, :]),
            tensor_ref[k],
            last,
            preferred_element_type=f32,
        )
        to_first = which(a, k) == 0
        sums[0] = sums[0] + jnp.where(to_first, part, 0.0)
        sums[1] = sums[1] + jnp.where(to_first, 0.0, part)
    width = ri_rows * TILE
    row = lax.broadcasted_iota(jnp.int32, (half, width), 0)
    col = lax.broadcasted_iota(jnp.int32, (half, width), 1)
    same = (row & (TILE - 1)) == (col & (TILE - 1))
    traces = jnp.concatenate(
        [jnp.where(same, s, 0.0).reshape(count, TILE, width).sum(axis=1) for s in sums], axis=0
    )
    pick = (
        lax.shift_right_logical(lax.broadcasted_iota(jnp.int32, (ri_rows, width), 1), jnp.int32(4))
        == lax.broadcasted_iota(jnp.int32, (ri_rows, width), 0)
    ).astype(f32)
    by_source = lax.dot_general(
        pick, traces, last, precision=lax.Precision.HIGHEST, preferred_element_type=f32
    )
    source = lax.broadcasted_iota(jnp.int32, (2 * count, 2 * count), 0)
    target = lax.broadcasted_iota(jnp.int32, (2 * count, 2 * count), 1)
    place = ((jnp.where(source < count, source, source - count) ^ r) * 2 + (source >= count).astype(jnp.int32)) == target
    ordered = jnp.dot(
        by_source, place.astype(f32), precision=lax.Precision.HIGHEST, preferred_element_type=f32
    )
    out_ref[...] = ordered * (1.0 / (ao * block))


def room(*arrays):
    total = sum(2 * math.prod(shape) for shape in arrays)
    return pltpu.CompilerParams(vmem_limit_bytes=min(2 * total + (4 << 20), 60 << 20))


def exchange(value, axis, size, k):
    return lax.ppermute(value, axis, [(i, i ^ k) for i in range(size)])


def shards(ri, ao, three_center, slab_tensor, occ_green, virt_green, pattern, atom_sizes):
    block = occ_green.shape[0]
    total = occ_green.shape[1]
    ri_rows = three_center.shape[0]
    atoms = pattern.shape[0]
    half = total + TILE
    bf16 = jnp.bfloat16
    vmem = pl.BlockSpec(memory_space=pltpu.VMEM)
    inputs = tuple(
        pltpu.with_memory_space_constraint(x, pltpu.HBM)
        for x in (atom_sizes.reshape(1, atoms), pattern, slab_tensor, occ_green, virt_green)
    )
    pay, green, green_part, screen = pl.pallas_call(
        prep_kernel,
        out_shape=(
            jax.ShapeDtypeStruct((half, block), bf16),
            jax.ShapeDtypeStruct((half, block), bf16),
            jax.ShapeDtypeStruct((total // 2 + TILE, block), bf16),
            jax.ShapeDtypeStruct((block, total), bf16),
        ),
        in_specs=[pl.BlockSpec(memory_space=pltpu.HBM)] * 5,
        out_specs=(vmem,) * 4,
        scratch_shapes=[pltpu.VMEM(x.shape, x.dtype) for x in inputs]
        + [pltpu.VMEM((block, total), bf16), pltpu.SemaphoreType.DMA((5,))],
        compiler_params=room((4 * half, block), (3 * block, total), (2 * block, 2 * total)),
        name="prep",
    )(*inputs)
    green_mine = [exchange(green_part, "ao", ao, k) for k in range(1, ao)]
    pays = [pay] + [exchange(pay, "ao", ao, k) for k in range(1, ao)]
    groups = block // TILE
    staged = pl.pallas_call(
        stage_kernel,
        out_shape=jax.ShapeDtypeStruct((ao, ri_rows * TILE, groups * block), bf16),
        in_specs=[pl.BlockSpec(memory_space=pltpu.HBM)] * 2,
        out_specs=vmem,
        scratch_shapes=[pltpu.VMEM(three_center.shape, bf16), pltpu.SemaphoreType.DMA],
        compiler_params=room((2 * ri_rows, block, total)),
        cost_estimate=pl.CostEstimate(flops=0, transcendentals=0, bytes_accessed=8 * ri_rows * block * total),
        name="stage",
    )(pltpu.with_memory_space_constraint(three_center, pltpu.HBM), pay)
    green_mine, staged = lax.optimization_barrier((green_mine, staged))
    green_other = [exchange(value, "ri", ri, 1) for value in green_mine]
    weighted = pl.pallas_call(
        lambda *refs: transform_kernel(ao, block, *refs),
        out_shape=jax.ShapeDtypeStruct((half, block), bf16),
        in_specs=[vmem] * (3 * ao) + [pl.BlockSpec(memory_space=pl.ANY)],
        out_specs=vmem,
        scratch_shapes=[
            pltpu.VMEM((2, total, total), bf16),
            pltpu.VMEM((ao, block, 2 * total), bf16),
            pltpu.VMEM((2, block, 2 * total), bf16),
        ],
        compiler_params=room((2 * half * ao, block), (2, total, total), (ao, block, 2 * total), (4, block, total)),
        name="transform",
    )(*pays, green, *green_mine, *green_other, screen, staged)
    sources = [weighted]
    for k in range(2, ri, 2):
        sources.append(exchange(weighted, "ri", ri, k))
    arrived = []
    for value in sources:
        arrived.append(value)
        arrived.append(exchange(value, "ri", ri, 1))
    part = pl.pallas_call(
        lambda *refs: contract_kernel(ri, ao, block, *refs),
        out_shape=jax.ShapeDtypeStruct((ri_rows, 2 * ri), jnp.float32),
        in_specs=[vmem] * (ri + 1),
        out_specs=vmem,
        compiler_params=room((half * ri, block), (2 * ri_rows, block, total)),
        name="contract",
    )(*arrived, staged)
    parts = [part] + [exchange(part, "ao", ao, k) for k in range(1, ao)]
    while len(parts) > 1:
        parts = [parts[i] + parts[i + 1] for i in range(0, len(parts), 2)]
    return parts[0]


def solution(mesh):
    placed = (P("ri", "ao", None), P("ri", "ao", None), P("ao", None), P("ao", None), P(), P())
    ri, ao = mesh.shape["ri"], mesh.shape["ao"]

    def body(*args):
        return shards(ri, ao, *args)

    return jax.shard_map(body, mesh=mesh, in_specs=placed, out_specs=P("ri", None), check_vma=False)
```

```python
import math

import jax
import jax.numpy as jnp
from jax import lax
from jax.experimental import pallas as pl
from jax.experimental.pallas import tpu as pltpu
from jax.sharding import PartitionSpec as P


ATOM_BS = 16
TILE = 16


def top_bit(k):
    return k.bit_length() - 1


def shared(k, ao):
    return ao == 4 and k == 3


def which(a, k):
    return lax.shift_right_logical(a, jnp.int32(top_bit(k))) & 1


def tri_masks(block):
    row = lax.broadcasted_iota(jnp.int32, (block, block), 0)
    col = lax.broadcasted_iota(jnp.int32, (block, block), 1)
    return row > col, row == col


def fold_diagonal(first, second, below, on):
    folded = jnp.where(below | on, first, second)
    diagonal = jnp.sum(jnp.where(on, second, 0.0), axis=0, keepdims=True)
    return folded, diagonal


def block_at(ref, index, block):
    return ref[:, pl.ds(pl.multiple_of(index * block, block), block)]


def prep_kernel(*refs):
    hbm, outs, copied, mask_ref, sems = refs[:5], refs[5:-7], refs[-7:-2], refs[-2], refs[-1]
    own_ref, screen_ref, pay_refs = outs[0], outs[1], outs[2:]
    copies = [pltpu.make_async_copy(src, dst, sems.at[i]) for i, (src, dst) in enumerate(zip(hbm, copied))]
    for copy in copies:
        copy.start()
    sizes_ref, pattern_ref, slab_ref, occ_ref, virt_ref = copied
    block = occ_ref.shape[0]
    total = occ_ref.shape[1]
    ao = total // block
    atoms = pattern_ref.shape[0]
    f32, bf16 = jnp.float32, jnp.bfloat16
    a = lax.axis_index("ao")
    row_atom = lax.shift_right_logical(
        lax.broadcasted_iota(jnp.int32, (block, atoms), 0), jnp.int32(4)
    ) + a * (block // ATOM_BS)
    pick_row = row_atom == lax.broadcasted_iota(jnp.int32, (block, atoms), 1)
    col_atom = lax.shift_right_logical(
        lax.broadcasted_iota(jnp.int32, (atoms, total), 1), jnp.int32(4)
    )
    pick_col = (col_atom == lax.broadcasted_iota(jnp.int32, (atoms, total), 0)).astype(f32).astype(bf16)
    copies[0].wait()
    copies[1].wait()
    sizes = sizes_ref[...].astype(f32)
    size_row = jnp.sum(jnp.where(pick_row, jnp.broadcast_to(sizes, (block, atoms)), 0.0), axis=1, keepdims=True)
    size_col = jnp.dot(
        jnp.broadcast_to(sizes, (8, atoms)).astype(bf16), pick_col, preferred_element_type=f32
    )[0:1]
    rows = jnp.dot(
        pick_row.astype(f32).astype(bf16), pattern_ref[...].astype(f32).astype(bf16),
        preferred_element_type=f32,
    ).astype(bf16)
    kept = jnp.dot(rows, pick_col, preferred_element_type=f32)
    slot_row = (lax.broadcasted_iota(jnp.int32, (block, total), 0) & (ATOM_BS - 1)).astype(f32)
    slot_col = (lax.broadcasted_iota(jnp.int32, (block, total), 1) & (ATOM_BS - 1)).astype(f32)
    live = (slot_row < size_row) & (slot_col < size_col)
    mask_ref[...] = jnp.where(live, kept, 0.0).astype(bf16)
    below, on = tri_masks(block)
    for copy in copies[2:]:
        copy.wait()
    slab_blocks, green_blocks = [], []
    for k in range(ao):
        screen = block_at(mask_ref, a ^ k, block)
        span = slice(k * block, (k + 1) * block)
        screen_ref[:, span] = screen
        cols = pl.ds(pl.multiple_of((a ^ k) * block, block), block)
        slabs = [slab_ref[q, :, cols] * screen for q in range(2)]
        greens = [occ_ref[:, cols], virt_ref[:, cols]]
        own_ref[0, :, span], own_ref[1, :, span] = slabs
        own_ref[2, :, span], own_ref[3, :, span] = greens
        if k == 0:
            folded = [fold_diagonal(x.astype(f32), y.astype(f32), below, on) for x, y in (slabs, greens)]
        else:
            first = which(a, k) == 0
            slab_blocks.append(jnp.where(first, *slabs))
            green_blocks.append(jnp.where(first, *greens))
    tails = []
    for (block_part, diagonal), blocks in zip(folded, (slab_blocks, green_blocks)):
        blocks.append(block_part.astype(bf16))
        tails.append(jnp.broadcast_to(diagonal, (TILE, block)).astype(bf16))

    def put(ref, at, parts, tail):
        for part in parts + [tail]:
            ref[at : at + part.shape[0], :] = part
            at += part.shape[0]
        return at

    even = (lax.axis_index("ri") & 1) == 0
    rows = block // 2
    for k in range(1, ao):
        at = put(pay_refs[k - 1], 0, slab_blocks[: k - 1] + slab_blocks[k:], tails[0])
        parts = green_blocks[: k - 1] + green_blocks[k:]
        if shared(k, ao):
            parts = [jnp.where(even, x[:rows], x[rows:]) for x in parts]
        put(pay_refs[k - 1], at, parts, tails[1])


def reader(ref, base, m, ao, block):
    def read(k):
        if k < 0:
            return ref[base + (ao - 1) * block : base + (ao - 1) * block + TILE, :]
        at = base + ((ao - 2) if k == 0 else k - 1 - (k > m)) * block
        return ref[at : at + block, :]

    return read


def halves_reader(mine, other, even, base, m, ao, block):
    here, there = (reader(x, base, m, ao, block // 2) for x in (mine, other))

    def read(k):
        if k < 0:
            return here(k)
        x, y = here(k), there(k)
        return jnp.concatenate([jnp.where(even, x, y), jnp.where(even, y, x)], axis=0)

    return read


def unfold(reads, own, a, ao, block, put):
    below, on = tri_masks(block)
    for q in range(2):
        for k in range(ao):
            value = own(q, k)
            put(q, 0, k, value)
            if k:
                put(q, k, 0, value.T)
    for m in range(1, ao):
        for j in range(m + 1, ao):
            k = m ^ j
            here = reads[m](k)
            there = reads[j](k)
            here_t = here.T
            there_t = there.T
            lower = which(a ^ m, k) == 0
            put(0, m, j, jnp.where(lower, here, there_t))
            put(0, j, m, jnp.where(lower, here_t, there))
            put(1, m, j, jnp.where(lower, there_t, here))
            put(1, j, m, jnp.where(lower, there, here_t))
        folded = reads[m](0).astype(jnp.float32)
        folded_t = folded.T
        diagonal = reads[m](-1).astype(jnp.float32)[0:1]
        put(0, m, m, jnp.where(below | on, folded, folded_t).astype(jnp.bfloat16))
        put(
            1, m, m,
            jnp.where(below, folded_t, jnp.where(on, jnp.broadcast_to(diagonal, (block, block)), folded)).astype(
                jnp.bfloat16
            ),
        )


def transform_kernel(ao, block, *refs):
    own_ref, screen_ref, _, out_ref, slab_ref, green_ref, left_ref = refs[-7:]
    pays = refs[:-7]
    total = ao * block
    a = lax.axis_index("ao")
    f32, bf16 = jnp.float32, jnp.bfloat16
    size = (ao - 1) * block + TILE
    pays, others = pays[: ao - 1], list(pays[ao - 1 :])
    even = (lax.axis_index("ri") & 1) == 0
    slabs, greens = [None], [None]
    for m, x in enumerate(pays, 1):
        slabs.append(reader(x, 0, m, ao, block))
        if shared(m, ao):
            greens.append(halves_reader(x, others.pop(0), even, size, m, ao, block))
        else:
            greens.append(reader(x, size, m, ao, block))

    def put_slab(matrix, row, col, value):
        slab_ref[matrix, row * block : (row + 1) * block, col * block : (col + 1) * block] = value

    def put_green(matrix, row, col, value):
        at = (total if matrix == 0 else 0) + col * block
        green_ref[row, :, at : at + block] = value

    def own(first):
        return lambda q, k: own_ref[first + q, :, k * block : (k + 1) * block]

    unfold(greens, own(2), a, ao, block, put_green)
    unfold(slabs, own(0), a, ao, block, put_slab)
    both = jnp.concatenate([green_ref[0, :, total:], green_ref[0, :, :total]], axis=0)
    for q in range(2):
        left = jnp.dot(both, slab_ref[q], preferred_element_type=f32).astype(bf16)
        left_ref[q, :, :total] = left[:block]
        left_ref[q, :, total:] = left[block:]
    last = (((1,), (1,)), ((), ()))
    for k in range(1, ao):
        sums = lax.dot_general(left_ref[which(a, k)], green_ref[k], last, preferred_element_type=f32)
        screen = screen_ref[:, k * block : (k + 1) * block].astype(f32)
        out_ref[(k - 1) * block : k * block, :] = (sums * screen).astype(bf16)
    below, on = tri_masks(block)
    weight = jnp.where(on, 0.5, 1.0) * screen_ref[:, 0:block].astype(f32)
    first, second = (
        lax.dot_general(left_ref[q], green_ref[0], last, preferred_element_type=f32) * weight for q in range(2)
    )
    folded, diagonal = fold_diagonal(first, second, below, on)
    at = (ao - 1) * block
    out_ref[at : at + block, :] = folded.astype(bf16)
    out_ref[at + block : at + block + TILE, :] = jnp.broadcast_to(diagonal, (TILE, block)).astype(bf16)


def stage_kernel(tensor_hbm, _, out_ref, tensor_ref, sem):
    ri_rows, block, _ = tensor_ref.shape
    a = lax.axis_index("ao")
    copy = pltpu.make_async_copy(tensor_hbm, tensor_ref, sem)
    copy.start()
    copy.wait()
    for k in range(out_ref.shape[0]):
        cols = pl.ds(pl.multiple_of((a ^ k) * block, block), block)
        for g in range(block // TILE):
            for p in range(ri_rows):
                out_ref[k, p * TILE : (p + 1) * TILE, g * block : (g + 1) * block] = tensor_ref[
                    p, g * TILE : (g + 1) * TILE, cols
                ]


def contract_kernel(count, ao, block, *refs):
    pays = refs[:count]
    tensor_ref, out_ref = refs[count:]
    ri_rows = tensor_ref.shape[1] // TILE
    a = lax.axis_index("ao")
    r = lax.axis_index("ri")
    f32, bf16 = jnp.float32, jnp.bfloat16
    groups = block // TILE
    last = (((1,), (1,)), ((), ()))

    def spread(values, rows_of):
        return jnp.concatenate(
            [
                jnp.concatenate([rows_of(v, slice(g * TILE, (g + 1) * TILE)) for v in values], axis=0)
                for g in range(groups)
            ],
            axis=1,
        )

    below, on = tri_masks(block)
    at = (ao - 1) * block
    firsts, seconds = [], []
    for pay in pays:
        folded = pay[at : at + block, :].astype(f32)
        diagonal = pay[at + block : at + block + TILE, :].astype(f32)[0:1]
        firsts.append(jnp.where(below | on, folded, 0.0).astype(bf16))
        seconds.append(
            jnp.where(below, 0.0, jnp.where(on, jnp.broadcast_to(diagonal, (block, block)), folded)).astype(bf16)
        )
    sums = lax.dot_general(
        spread(firsts + seconds, lambda v, rows: v[rows]), tensor_ref[0], last, preferred_element_type=f32
    )
    half = count * TILE
    sums = [sums[:half], sums[half:]]
    for k in range(1, ao):
        start = (k - 1) * block
        part = lax.dot_general(
            spread(pays, lambda pay, rows: pay[start + rows.start : start + rows.stop, :]),
            tensor_ref[k],
            last,
            preferred_element_type=f32,
        )
        to_first = which(a, k) == 0
        sums[0] = sums[0] + jnp.where(to_first, part, 0.0)
        sums[1] = sums[1] + jnp.where(to_first, 0.0, part)
    width = ri_rows * TILE
    row = lax.broadcasted_iota(jnp.int32, (half, width), 0)
    col = lax.broadcasted_iota(jnp.int32, (half, width), 1)
    same = (row & (TILE - 1)) == (col & (TILE - 1))
    traces = jnp.concatenate(
        [jnp.where(same, s, 0.0).reshape(count, TILE, width).sum(axis=1) for s in sums], axis=0
    )
    pick = (
        lax.shift_right_logical(lax.broadcasted_iota(jnp.int32, (ri_rows, width), 1), jnp.int32(4))
        == lax.broadcasted_iota(jnp.int32, (ri_rows, width), 0)
    ).astype(f32)
    by_source = lax.dot_general(
        pick, traces, last, precision=lax.Precision.HIGHEST, preferred_element_type=f32
    )
    source = lax.broadcasted_iota(jnp.int32, (2 * count, 2 * count), 0)
    target = lax.broadcasted_iota(jnp.int32, (2 * count, 2 * count), 1)
    place = ((jnp.where(source < count, source, source - count) ^ r) * 2 + (source >= count).astype(jnp.int32)) == target
    ordered = jnp.dot(
        by_source, place.astype(f32), precision=lax.Precision.HIGHEST, preferred_element_type=f32
    )
    out_ref[...] = ordered * (1.0 / (ao * block))


def room(*arrays):
    total = sum(2 * math.prod(shape) for shape in arrays)
    return pltpu.CompilerParams(vmem_limit_bytes=min(2 * total + (4 << 20), 60 << 20))


def exchange(value, axis, size, k):
    return lax.ppermute(value, axis, [(i, i ^ k) for i in range(size)])


def shards(ri, ao, three_center, slab_tensor, occ_green, virt_green, pattern, atom_sizes):
    block = occ_green.shape[0]
    total = occ_green.shape[1]
    ri_rows = three_center.shape[0]
    atoms = pattern.shape[0]
    half = total + TILE
    bf16 = jnp.bfloat16
    vmem = pl.BlockSpec(memory_space=pltpu.VMEM)
    inputs = tuple(
        pltpu.with_memory_space_constraint(x, pltpu.HBM)
        for x in (atom_sizes.reshape(1, atoms), pattern, slab_tensor, occ_green, virt_green)
    )
    size = (ao - 1) * block + TILE
    sizes = [size + (size - (ao - 1) * block // 2 if shared(k, ao) else size) for k in range(1, ao)]
    prepared = pl.pallas_call(
        prep_kernel,
        out_shape=[jax.ShapeDtypeStruct((4, block, total), bf16), jax.ShapeDtypeStruct((block, total), bf16)]
        + [jax.ShapeDtypeStruct((rows, block), bf16) for rows in sizes],
        in_specs=[pl.BlockSpec(memory_space=pltpu.HBM)] * 5,
        out_specs=[vmem] * (2 + len(sizes)),
        scratch_shapes=[pltpu.VMEM(x.shape, x.dtype) for x in inputs]
        + [pltpu.VMEM((block, total), bf16), pltpu.SemaphoreType.DMA((5,))],
        compiler_params=room((sum(sizes), block), (5 * block, total), (2 * block, 2 * total)),
        name="prep",
    )(*inputs)
    own, screen, *pays = prepared
    arrived = []
    for k, pay in enumerate(pays, 1):
        arrived.append(exchange(pay, "ao", ao, k))
    pays = arrived + [exchange(x, "ri", ri, 1) for k, x in enumerate(arrived, 1) if shared(k, ao)]
    groups = block // TILE
    staged = pl.pallas_call(
        stage_kernel,
        out_shape=jax.ShapeDtypeStruct((ao, ri_rows * TILE, groups * block), bf16),
        in_specs=[pl.BlockSpec(memory_space=pltpu.HBM)] * 2,
        out_specs=vmem,
        scratch_shapes=[pltpu.VMEM(three_center.shape, bf16), pltpu.SemaphoreType.DMA],
        compiler_params=room((2 * ri_rows, block, total)),
        cost_estimate=pl.CostEstimate(flops=0, transcendentals=0, bytes_accessed=8 * ri_rows * block * total),
        name="stage",
    )(pltpu.with_memory_space_constraint(three_center, pltpu.HBM), screen)
    weighted = pl.pallas_call(
        lambda *refs: transform_kernel(ao, block, *refs),
        out_shape=jax.ShapeDtypeStruct((half, block), bf16),
        in_specs=[vmem] * (len(pays) + 2) + [pl.BlockSpec(memory_space=pl.ANY)],
        out_specs=vmem,
        scratch_shapes=[
            pltpu.VMEM((2, total, total), bf16),
            pltpu.VMEM((ao, block, 2 * total), bf16),
            pltpu.VMEM((2, block, 2 * total), bf16),
        ],
        compiler_params=room((sum(sizes), block), (4 * block, total), (2, total, total), (ao, block, 2 * total), (4, block, total)),
        name="transform",
    )(*pays, own, screen, staged)
    sources = [weighted]
    for k in range(2, ri, 2):
        sources.append(exchange(weighted, "ri", ri, k))
    arrived = []
    for value in sources:
        arrived.append(value)
        arrived.append(exchange(value, "ri", ri, 1))
    part = pl.pallas_call(
        lambda *refs: contract_kernel(ri, ao, block, *refs),
        out_shape=jax.ShapeDtypeStruct((ri_rows, 2 * ri), jnp.float32),
        in_specs=[vmem] * (ri + 1),
        out_specs=vmem,
        compiler_params=room((half * ri, block), (2 * ri_rows, block, total)),
        name="contract",
    )(*arrived, staged)
    parts = [part] + [exchange(part, "ao", ao, k) for k in range(1, ao)]
    while len(parts) > 1:
        parts = [parts[i] + parts[i + 1] for i in range(0, len(parts), 2)]
    return parts[0]


def solution(mesh):
    placed = (P("ri", "ao", None), P("ri", "ao", None), P("ao", None), P("ao", None), P(), P())
    ri, ao = mesh.shape["ri"], mesh.shape["ao"]

    def body(*args):
        return shards(ri, ao, *args)

    return jax.shard_map(body, mesh=mesh, in_specs=placed, out_specs=P("ri", None), check_vma=False)
```

```python
import math

import jax
import jax.numpy as jnp
from jax import lax
from jax.experimental import pallas as pl
from jax.experimental.pallas import tpu as pltpu
from jax.sharding import PartitionSpec as P


ATOM_BS = 16
TILE = 16
TAIL = 8


def top_bit(k):
    return k.bit_length() - 1


def shared(k, ao):
    return ao == 4 and k == 3


def which(a, k):
    return lax.shift_right_logical(a, jnp.int32(top_bit(k))) & 1


def tri_masks(block):
    row = lax.broadcasted_iota(jnp.int32, (block, block), 0)
    col = lax.broadcasted_iota(jnp.int32, (block, block), 1)
    return row > col, row == col


def fold_diagonal(first, second, below, on):
    folded = jnp.where(below | on, first, second)
    diagonal = jnp.sum(jnp.where(on, second, 0.0), axis=0, keepdims=True)
    return folded, diagonal


def block_at(ref, index, block):
    return ref[:, pl.ds(pl.multiple_of(index * block, block), block)]


def pieces(shape):
    half = shape[-2] // 2
    halves = [pl.ds(0, half), pl.ds(half, half)]
    return halves if len(shape) == 2 else [(i, x) for i in range(shape[0]) for x in halves]


def prep_kernel(*refs):
    hbm, outs, copied, mask_ref, sems = refs[:5], refs[5:-7], refs[-7:-2], refs[-2], refs[-1]
    own_ref, screen_ref, pay_refs = outs[0], outs[1], outs[2:]
    copies = []
    for i, (src, dst) in enumerate(zip(hbm, copied)):
        parts = [(src, dst)] if i < 2 else [(src.at[x], dst.at[x]) for x in pieces(src.shape)]
        copies += [pltpu.make_async_copy(x, y, sems.at[len(copies) + n]) for n, (x, y) in enumerate(parts)]
    for copy in copies:
        copy.start()
    sizes_ref, pattern_ref, slab_ref, occ_ref, virt_ref = copied
    block = occ_ref.shape[0]
    total = occ_ref.shape[1]
    ao = total // block
    atoms = pattern_ref.shape[0]
    f32, bf16 = jnp.float32, jnp.bfloat16
    a = lax.axis_index("ao")
    row_atom = lax.shift_right_logical(
        lax.broadcasted_iota(jnp.int32, (block, atoms), 0), jnp.int32(4)
    ) + a * (block // ATOM_BS)
    pick_row = row_atom == lax.broadcasted_iota(jnp.int32, (block, atoms), 1)
    col_atom = lax.shift_right_logical(
        lax.broadcasted_iota(jnp.int32, (atoms, total), 1), jnp.int32(4)
    )
    pick_col = (col_atom == lax.broadcasted_iota(jnp.int32, (atoms, total), 0)).astype(f32).astype(bf16)
    copies[0].wait()
    copies[1].wait()
    sizes = sizes_ref[...].astype(f32)
    size_row = jnp.sum(jnp.where(pick_row, jnp.broadcast_to(sizes, (block, atoms)), 0.0), axis=1, keepdims=True)
    size_col = jnp.dot(
        jnp.broadcast_to(sizes, (8, atoms)).astype(bf16), pick_col, preferred_element_type=f32
    )[0:1]
    rows = jnp.dot(
        pick_row.astype(f32).astype(bf16), pattern_ref[...].astype(f32).astype(bf16),
        preferred_element_type=f32,
    ).astype(bf16)
    kept = jnp.dot(rows, pick_col, preferred_element_type=f32)
    slot_row = (lax.broadcasted_iota(jnp.int32, (block, total), 0) & (ATOM_BS - 1)).astype(f32)
    slot_col = (lax.broadcasted_iota(jnp.int32, (block, total), 1) & (ATOM_BS - 1)).astype(f32)
    live = (slot_row < size_row) & (slot_col < size_col)
    mask_ref[...] = jnp.where(live, kept, 0.0).astype(bf16)
    below, on = tri_masks(block)
    for copy in copies[2:]:
        copy.wait()
    slab_blocks, green_blocks = [], []
    for k in range(ao):
        screen = block_at(mask_ref, a ^ k, block)
        span = slice(k * block, (k + 1) * block)
        screen_ref[:, span] = screen
        cols = pl.ds(pl.multiple_of((a ^ k) * block, block), block)
        slabs = [slab_ref[q, :, cols] * screen for q in range(2)]
        greens = [occ_ref[:, cols], virt_ref[:, cols]]
        own_ref[0, :, span], own_ref[1, :, span] = slabs
        own_ref[2, :, span], own_ref[3, :, span] = greens
        if k == 0:
            folded = [fold_diagonal(x.astype(f32), y.astype(f32), below, on) for x, y in (slabs, greens)]
        else:
            first = which(a, k) == 0
            slab_blocks.append(jnp.where(first, *slabs))
            green_blocks.append(jnp.where(first, *greens))
    slab_blocks.append(folded[0][0].astype(bf16))
    green_blocks.append(folded[1][0].astype(bf16))
    upper = lax.broadcasted_iota(jnp.int32, (2 * TAIL, block), 0) < TAIL
    tail = jnp.where(upper, folded[0][1], folded[1][1]).astype(bf16)

    even = (lax.axis_index("ri") & 1) == 0
    rows = block // 2
    for k in range(1, ao):
        parts = green_blocks[: k - 1] + green_blocks[k:]
        if shared(k, ao):
            parts = [jnp.where(even, x[:rows], x[rows:]) for x in parts]
        at = 0
        for part in slab_blocks[: k - 1] + slab_blocks[k:] + parts + [tail]:
            pay_refs[k - 1][at : at + part.shape[0], :] = part
            at += part.shape[0]


def reader(ref, base, m, ao, block):
    def read(k):
        at = base + ((ao - 2) if k == 0 else k - 1 - (k > m)) * block
        return ref[at : at + block, :]

    return read


def halves_reader(mine, other, even, base, m, ao, block):
    here, there = (reader(x, base, m, ao, block // 2) for x in (mine, other))

    def read(k):
        x, y = here(k), there(k)
        return jnp.concatenate([jnp.where(even, x, y), jnp.where(even, y, x)], axis=0)

    return read


def unfold(reads, diagonals, own, a, ao, block, put):
    below, on = tri_masks(block)
    for q in range(2):
        for k in range(ao):
            value = own(q, k)
            put(q, 0, k, value)
            if k:
                put(q, k, 0, value.T)
    for m in range(1, ao):
        for k in range(1, ao):
            if k != m:
                value = reads[m](k)
                put(which(a ^ m, k), m, m ^ k, value)
                put(which(a ^ m, k), m ^ k, m, value.T)
        folded = reads[m](0).astype(jnp.float32)
        folded_t = folded.T
        diagonal = diagonals[m]
        put(0, m, m, jnp.where(below | on, folded, folded_t).astype(jnp.bfloat16))
        put(
            1, m, m,
            jnp.where(below, folded_t, jnp.where(on, jnp.broadcast_to(diagonal, (block, block)), folded)).astype(
                jnp.bfloat16
            ),
        )


def transform_kernel(ao, block, *refs):
    own_ref, screen_ref, _, out_ref, slab_ref, green_ref, left_ref = refs[-7:]
    pays = refs[:-7]
    total = ao * block
    a = lax.axis_index("ao")
    f32, bf16 = jnp.float32, jnp.bfloat16
    size = (ao - 1) * block
    pays, others = pays[: ao - 1], list(pays[ao - 1 :])
    even = (lax.axis_index("ri") & 1) == 0
    slabs, greens, diagonals = [None], [None], ([None], [None])
    for m, x in enumerate(pays, 1):
        tail = x[x.shape[0] - 2 * TAIL :, :].astype(f32)
        for rows, at in zip(diagonals, (0, TAIL)):
            rows.append(tail[at : at + 1])
        slabs.append(reader(x, 0, m, ao, block))
        if shared(m, ao):
            greens.append(halves_reader(x, others.pop(0), even, size, m, ao, block))
        else:
            greens.append(reader(x, size, m, ao, block))

    def put_slab(matrix, row, col, value):
        slab_ref[matrix, row * block : (row + 1) * block, col * block : (col + 1) * block] = value

    def put_green(matrix, row, col, value):
        at = pl.multiple_of((1 - matrix) * total + col * block, block)
        green_ref[row, :, pl.ds(at, block)] = value

    def own(first):
        return lambda q, k: own_ref[first + q, :, k * block : (k + 1) * block]

    unfold(greens, diagonals[1], own(2), a, ao, block, put_green)
    unfold(slabs, diagonals[0], own(0), a, ao, block, put_slab)
    both = jnp.concatenate([green_ref[0, :, total:], green_ref[0, :, :total]], axis=0)
    for q in range(2):
        left = jnp.dot(both, slab_ref[q], preferred_element_type=f32).astype(bf16)
        left_ref[q, :, :total] = left[:block]
        left_ref[q, :, total:] = left[block:]
    last = (((1,), (1,)), ((), ()))
    below, on = tri_masks(block)

    def put_block(k, sums):
        screen = screen_ref[:, k * block : (k + 1) * block].astype(f32)
        out_ref[(k - 1) * block : k * block, :] = (sums * screen).astype(bf16)

    lefts = jnp.concatenate([left_ref[0], left_ref[1]], axis=0)
    rights = green_ref[0 : min(2, ao)].reshape(min(2, ao) * block, 2 * total)
    sums = lax.dot_general(lefts, rights, last, preferred_element_type=f32)
    weight = jnp.where(on, 0.5, 1.0) * screen_ref[:, 0:block].astype(f32)
    folded, diagonal = fold_diagonal(sums[:block, :block] * weight, sums[block:, :block] * weight, below, on)
    if ao > 1:
        put_block(1, jnp.where(which(a, 1) == 0, sums[:block, block:], sums[block:, block:]))
    start = 2
    while start < ao:
        rights = green_ref[start : 2 * start].reshape(start * block, 2 * total)
        sums = lax.dot_general(left_ref[which(a, start)], rights, last, preferred_element_type=f32)
        for k in range(start, 2 * start):
            put_block(k, sums[:, (k - start) * block : (k - start + 1) * block])
        start *= 2
    at = (ao - 1) * block
    out_ref[at : at + block, :] = folded.astype(bf16)
    out_ref[at + block :, :] = jnp.broadcast_to(diagonal, (TAIL, block)).astype(bf16)


def stage_kernel(tensor_hbm, _, out_ref, tensor_ref, rows_ref, sem):
    ri_rows, block, _ = tensor_ref.shape
    a = lax.axis_index("ao")
    copy = pltpu.make_async_copy(tensor_hbm, tensor_ref, sem)
    copy.start()
    copy.wait()
    for k in range(out_ref.shape[0]):
        cols = pl.ds(pl.multiple_of((a ^ k) * block, block), block)
        for g in range(block // TILE):
            for p in range(ri_rows):
                rows_ref[p * TILE : (p + 1) * TILE, :] = tensor_ref[p, g * TILE : (g + 1) * TILE, cols]
            out_ref[k, g * block : (g + 1) * block, :] = rows_ref[...].T


def contract_kernel(count, ao, block, *refs):
    pays = refs[:count]
    tensor_ref, out_ref = refs[count:]
    ri_rows = tensor_ref.shape[2] // TILE
    a = lax.axis_index("ao")
    r = lax.axis_index("ri")
    f32, bf16 = jnp.float32, jnp.bfloat16
    groups = block // TILE
    last, plain = (((1,), (1,)), ((), ())), (((1,), (0,)), ((), ()))

    def spread(values, rows_of):
        return jnp.concatenate(
            [
                jnp.concatenate([rows_of(v, slice(g * TILE, (g + 1) * TILE)) for v in values], axis=0)
                for g in range(groups)
            ],
            axis=1,
        )

    below, on = tri_masks(block)
    at = (ao - 1) * block
    firsts, seconds = [], []
    for pay in pays:
        folded = pay[at : at + block, :].astype(f32)
        diagonal = pay[at + block : at + block + TAIL, :].astype(f32)[0:1]
        firsts.append(jnp.where(below | on, folded, 0.0).astype(bf16))
        seconds.append(
            jnp.where(below, 0.0, jnp.where(on, jnp.broadcast_to(diagonal, (block, block)), folded)).astype(bf16)
        )
    sums = lax.dot_general(
        spread(firsts + seconds, lambda v, rows: v[rows]), tensor_ref[0], plain, preferred_element_type=f32
    )
    half, width = count * TILE, ri_rows * TILE
    row = lax.broadcasted_iota(jnp.int32, (half, width), 0)
    col = lax.broadcasted_iota(jnp.int32, (half, width), 1)
    same = (row & (TILE - 1)) == (col & (TILE - 1))

    def trace(values):
        return jnp.where(same, values, 0.0).reshape(count, TILE, width).sum(axis=1)

    traces = [trace(sums[:half]), trace(sums[half:])]
    for k in range(1, ao):
        start = (k - 1) * block
        part = trace(
            lax.dot_general(
                spread(pays, lambda pay, rows: pay[start + rows.start : start + rows.stop, :]),
                tensor_ref[k],
                plain,
                preferred_element_type=f32,
            )
        )
        to_first = which(a, k) == 0
        traces[0] = traces[0] + jnp.where(to_first, part, 0.0)
        traces[1] = traces[1] + jnp.where(to_first, 0.0, part)
    traces = jnp.concatenate(traces, axis=0)
    pick = (
        lax.shift_right_logical(lax.broadcasted_iota(jnp.int32, (ri_rows, width), 1), jnp.int32(4))
        == lax.broadcasted_iota(jnp.int32, (ri_rows, width), 0)
    ).astype(f32)
    by_source = lax.dot_general(
        pick, traces, last, precision=lax.Precision.HIGHEST, preferred_element_type=f32
    )
    source = lax.broadcasted_iota(jnp.int32, (2 * count, 2 * count), 0)
    target = lax.broadcasted_iota(jnp.int32, (2 * count, 2 * count), 1)
    place = ((jnp.where(source < count, source, source - count) ^ r) * 2 + (source >= count).astype(jnp.int32)) == target
    ordered = jnp.dot(
        by_source, place.astype(f32), precision=lax.Precision.HIGHEST, preferred_element_type=f32
    )
    out_ref[...] = ordered * (1.0 / (ao * block))


def room(*arrays):
    total = sum(2 * math.prod(shape) for shape in arrays)
    return pltpu.CompilerParams(vmem_limit_bytes=min(2 * total + (4 << 20), 60 << 20))


def exchange(value, axis, size, k):
    return lax.ppermute(value, axis, [(i, i ^ k) for i in range(size)])


def shards(ri, ao, three_center, slab_tensor, occ_green, virt_green, pattern, atom_sizes):
    block = occ_green.shape[0]
    total = occ_green.shape[1]
    ri_rows = three_center.shape[0]
    atoms = pattern.shape[0]
    half = total + TAIL
    bf16 = jnp.bfloat16
    vmem = pl.BlockSpec(memory_space=pltpu.VMEM)
    inputs = tuple(
        pltpu.with_memory_space_constraint(x, pltpu.HBM)
        for x in (atom_sizes.reshape(1, atoms), pattern, slab_tensor, occ_green, virt_green)
    )
    size = (ao - 1) * block
    sizes = [size + (size // 2 if shared(k, ao) else size) + 2 * TAIL for k in range(1, ao)]
    prepared = pl.pallas_call(
        prep_kernel,
        out_shape=[jax.ShapeDtypeStruct((4, block, total), bf16), jax.ShapeDtypeStruct((block, total), bf16)]
        + [jax.ShapeDtypeStruct((rows, block), bf16) for rows in sizes],
        in_specs=[pl.BlockSpec(memory_space=pltpu.HBM)] * 5,
        out_specs=[vmem] * (2 + len(sizes)),
        scratch_shapes=[pltpu.VMEM(x.shape, x.dtype) for x in inputs]
        + [pltpu.VMEM((block, total), bf16), pltpu.SemaphoreType.DMA((2 + sum(len(pieces(x.shape)) for x in inputs[2:]),))],
        compiler_params=room((sum(sizes), block), (5 * block, total), (2 * block, 2 * total)),
        name="prep",
    )(*inputs)
    own, screen, *pays = prepared
    arrived = []
    for k, pay in enumerate(pays, 1):
        arrived.append(exchange(pay, "ao", ao, k))
    pays = arrived + [exchange(x, "ri", ri, 1) for k, x in enumerate(arrived, 1) if shared(k, ao)]
    groups = block // TILE
    staged = pl.pallas_call(
        stage_kernel,
        out_shape=jax.ShapeDtypeStruct((ao, groups * block, ri_rows * TILE), bf16),
        in_specs=[pl.BlockSpec(memory_space=pltpu.HBM)] * 2,
        out_specs=vmem,
        scratch_shapes=[
            pltpu.VMEM(three_center.shape, bf16),
            pltpu.VMEM((ri_rows * TILE, block), bf16),
            pltpu.SemaphoreType.DMA,
        ],
        compiler_params=room((2 * ri_rows, block, total)),
        cost_estimate=pl.CostEstimate(flops=0, transcendentals=0, bytes_accessed=8 * ri_rows * block * total),
        name="stage",
    )(pltpu.with_memory_space_constraint(three_center, pltpu.HBM), screen)
    weighted = pl.pallas_call(
        lambda *refs: transform_kernel(ao, block, *refs),
        out_shape=jax.ShapeDtypeStruct((half, block), bf16),
        in_specs=[vmem] * (len(pays) + 2) + [pl.BlockSpec(memory_space=pl.ANY)],
        out_specs=vmem,
        scratch_shapes=[
            pltpu.VMEM((2, total, total), bf16),
            pltpu.VMEM((ao, block, 2 * total), bf16),
            pltpu.VMEM((2, block, 2 * total), bf16),
        ],
        compiler_params=room((sum(sizes), block), (4 * block, total), (2, total, total), (ao, block, 2 * total), (4, block, total)),
        name="transform",
    )(*pays, own, screen, staged)
    sources = [weighted]
    for k in range(2, ri, 2):
        sources.append(exchange(weighted, "ri", ri, k))
    arrived = []
    for value in sources:
        arrived.append(value)
        arrived.append(exchange(value, "ri", ri, 1))
    part = pl.pallas_call(
        lambda *refs: contract_kernel(ri, ao, block, *refs),
        out_shape=jax.ShapeDtypeStruct((ri_rows, 2 * ri), jnp.float32),
        in_specs=[vmem] * (ri + 1),
        out_specs=vmem,
        compiler_params=room((half * ri, block), (2 * ri_rows, block, total)),
        name="contract",
    )(*arrived, staged)
    parts = [part] + [exchange(part, "ao", ao, k) for k in range(1, ao)]
    while len(parts) > 1:
        parts = [parts[i] + parts[i + 1] for i in range(0, len(parts), 2)]
    return parts[0]


def solution(mesh):
    placed = (P("ri", "ao", None), P("ri", "ao", None), P("ao", None), P("ao", None), P(), P())
    ri, ao = mesh.shape["ri"], mesh.shape["ao"]

    def body(*args):
        return shards(ri, ao, *args)

    return jax.shard_map(body, mesh=mesh, in_specs=placed, out_specs=P("ri", None), check_vma=False)
```

```python
import math

import jax
import jax.numpy as jnp
from jax import lax
from jax.experimental import pallas as pl
from jax.experimental.pallas import tpu as pltpu
from jax.sharding import PartitionSpec as P


ATOM_BS = 16
TILE = 16
TAIL = 8


def top_bit(k):
    return k.bit_length() - 1


def shared(k, ao):
    return ao == 4 and k == 3


def which(a, k):
    return lax.shift_right_logical(a, jnp.int32(top_bit(k))) & 1


def tri_masks(block):
    row = lax.broadcasted_iota(jnp.int32, (block, block), 0)
    col = lax.broadcasted_iota(jnp.int32, (block, block), 1)
    return row > col, row == col


def fold_diagonal(first, second, below, on):
    folded = jnp.where(below | on, first, second)
    diagonal = jnp.sum(jnp.where(on, second, 0.0), axis=0, keepdims=True)
    return folded, diagonal


def block_at(ref, index, block):
    return ref[:, pl.ds(pl.multiple_of(index * block, block), block)]


def pieces(shape):
    half = shape[-2] // 2
    halves = [pl.ds(0, half), pl.ds(half, half)]
    return halves if len(shape) == 2 else [(i, x) for i in range(shape[0]) for x in halves]


def prep_kernel(*refs):
    hbm, outs, copied, mask_ref, sems = refs[:5], refs[5:-7], refs[-7:-2], refs[-2], refs[-1]
    own_ref, screen_ref, pay_refs = outs[0], outs[1], outs[2:]
    copies = []
    for i, (src, dst) in enumerate(zip(hbm, copied)):
        parts = [(src, dst)] if i < 2 else [(src.at[x], dst.at[x]) for x in pieces(src.shape)]
        copies += [pltpu.make_async_copy(x, y, sems.at[len(copies) + n]) for n, (x, y) in enumerate(parts)]
    for copy in copies:
        copy.start()
    sizes_ref, pattern_ref, slab_ref, occ_ref, virt_ref = copied
    block = occ_ref.shape[0]
    total = occ_ref.shape[1]
    ao = total // block
    atoms = pattern_ref.shape[0]
    f32, bf16 = jnp.float32, jnp.bfloat16
    a = lax.axis_index("ao")
    row_atom = lax.shift_right_logical(
        lax.broadcasted_iota(jnp.int32, (block, atoms), 0), jnp.int32(4)
    ) + a * (block // ATOM_BS)
    pick_row = row_atom == lax.broadcasted_iota(jnp.int32, (block, atoms), 1)
    col_atom = lax.shift_right_logical(
        lax.broadcasted_iota(jnp.int32, (atoms, total), 1), jnp.int32(4)
    )
    pick_col = (col_atom == lax.broadcasted_iota(jnp.int32, (atoms, total), 0)).astype(f32).astype(bf16)
    copies[0].wait()
    copies[1].wait()
    sizes = sizes_ref[...].astype(f32)
    size_row = jnp.sum(jnp.where(pick_row, jnp.broadcast_to(sizes, (block, atoms)), 0.0), axis=1, keepdims=True)
    size_col = jnp.dot(
        jnp.broadcast_to(sizes, (8, atoms)).astype(bf16), pick_col, preferred_element_type=f32
    )[0:1]
    rows = jnp.dot(
        pick_row.astype(f32).astype(bf16), pattern_ref[...].astype(f32).astype(bf16),
        preferred_element_type=f32,
    ).astype(bf16)
    kept = jnp.dot(rows, pick_col, preferred_element_type=f32)
    slot_row = (lax.broadcasted_iota(jnp.int32, (block, total), 0) & (ATOM_BS - 1)).astype(f32)
    slot_col = (lax.broadcasted_iota(jnp.int32, (block, total), 1) & (ATOM_BS - 1)).astype(f32)
    live = (slot_row < size_row) & (slot_col < size_col)
    mask_ref[...] = jnp.where(live, kept, 0.0).astype(bf16)
    below, on = tri_masks(block)
    for copy in copies[2:]:
        copy.wait()
    slab_blocks, green_blocks = [], []
    for k in range(ao):
        screen = block_at(mask_ref, a ^ k, block)
        span = slice(k * block, (k + 1) * block)
        screen_ref[:, span] = screen
        cols = pl.ds(pl.multiple_of((a ^ k) * block, block), block)
        slabs = [slab_ref[q, :, cols] * screen for q in range(2)]
        greens = [occ_ref[:, cols], virt_ref[:, cols]]
        own_ref[0, :, span], own_ref[1, :, span] = slabs
        own_ref[2, :, span], own_ref[3, :, span] = greens
        if k == 0:
            folded = [fold_diagonal(x.astype(f32), y.astype(f32), below, on) for x, y in (slabs, greens)]
        else:
            first = which(a, k) == 0
            slab_blocks.append(jnp.where(first, *slabs))
            green_blocks.append(jnp.where(first, *greens))
    slab_blocks.append(folded[0][0].astype(bf16))
    green_blocks.append(folded[1][0].astype(bf16))
    upper = lax.broadcasted_iota(jnp.int32, (2 * TAIL, block), 0) < TAIL
    tail = jnp.where(upper, folded[0][1], folded[1][1]).astype(bf16)

    even = (lax.axis_index("ri") & 1) == 0
    rows = block // 2
    for k in range(1, ao):
        parts = green_blocks[: k - 1] + green_blocks[k:]
        if shared(k, ao):
            parts = [jnp.where(even, x[:rows], x[rows:]) for x in parts]
        at = 0
        for part in slab_blocks[: k - 1] + slab_blocks[k:] + parts + [tail]:
            pay_refs[k - 1][at : at + part.shape[0], :] = part
            at += part.shape[0]


def reader(ref, base, m, ao, block):
    def read(k):
        at = base + ((ao - 2) if k == 0 else k - 1 - (k > m)) * block
        return ref[at : at + block, :]

    return read


def halves_reader(mine, other, even, base, m, ao, block):
    here, there = (reader(x, base, m, ao, block // 2) for x in (mine, other))

    def read(k):
        x, y = here(k), there(k)
        return jnp.concatenate([jnp.where(even, x, y), jnp.where(even, y, x)], axis=0)

    return read


def unfold(reads, diagonals, own, a, ao, block, put):
    below, on = tri_masks(block)
    for q in range(2):
        for k in range(ao):
            value = own(q, k)
            put(q, 0, k, value)
            if k:
                put(q, k, 0, value.T)
    for m in range(1, ao):
        for k in range(1, ao):
            if k != m:
                value = reads[m](k)
                put(which(a ^ m, k), m, m ^ k, value)
                put(which(a ^ m, k), m ^ k, m, value.T)
        folded = reads[m](0).astype(jnp.float32)
        folded_t = folded.T
        diagonal = diagonals[m]
        put(0, m, m, jnp.where(below | on, folded, folded_t).astype(jnp.bfloat16))
        put(
            1, m, m,
            jnp.where(below, folded_t, jnp.where(on, jnp.broadcast_to(diagonal, (block, block)), folded)).astype(
                jnp.bfloat16
            ),
        )


def transform_kernel(ao, block, *refs):
    own_ref, screen_ref, _, out_ref, slab_ref, green_ref, left_ref = refs[-7:]
    pays = refs[:-7]
    total = ao * block
    a = lax.axis_index("ao")
    f32, bf16 = jnp.float32, jnp.bfloat16
    size = (ao - 1) * block
    pays, others = pays[: ao - 1], list(pays[ao - 1 :])
    even = (lax.axis_index("ri") & 1) == 0
    slabs, greens, diagonals = [None], [None], ([None], [None])
    for m, x in enumerate(pays, 1):
        tail = x[x.shape[0] - 2 * TAIL :, :].astype(f32)
        for rows, at in zip(diagonals, (0, TAIL)):
            rows.append(tail[at : at + 1])
        slabs.append(reader(x, 0, m, ao, block))
        if shared(m, ao):
            greens.append(halves_reader(x, others.pop(0), even, size, m, ao, block))
        else:
            greens.append(reader(x, size, m, ao, block))

    def put_slab(matrix, row, col, value):
        slab_ref[matrix, row * block : (row + 1) * block, col * block : (col + 1) * block] = value

    def put_green(matrix, row, col, value):
        at = pl.multiple_of((1 - matrix) * total + col * block, block)
        green_ref[row, :, pl.ds(at, block)] = value

    def own(first):
        return lambda q, k: own_ref[first + q, :, k * block : (k + 1) * block]

    unfold(greens, diagonals[1], own(2), a, ao, block, put_green)
    unfold(slabs, diagonals[0], own(0), a, ao, block, put_slab)
    both = jnp.concatenate([green_ref[0, :, total:], green_ref[0, :, :total]], axis=0)
    for q in range(2):
        left = jnp.dot(both, slab_ref[q], preferred_element_type=f32).astype(bf16)
        left_ref[q, :, :total] = left[:block]
        left_ref[q, :, total:] = left[block:]
    last = (((1,), (1,)), ((), ()))
    below, on = tri_masks(block)

    def put_block(k, sums):
        screen = screen_ref[:, k * block : (k + 1) * block].astype(f32)
        out_ref[(k - 1) * block : k * block, :] = (sums * screen).astype(bf16)

    lefts = jnp.concatenate([left_ref[0], left_ref[1]], axis=0)
    rights = green_ref[0 : min(2, ao)].reshape(min(2, ao) * block, 2 * total)
    sums = lax.dot_general(lefts, rights, last, preferred_element_type=f32)
    weight = jnp.where(on, 0.5, 1.0) * screen_ref[:, 0:block].astype(f32)
    folded, diagonal = fold_diagonal(sums[:block, :block] * weight, sums[block:, :block] * weight, below, on)
    if ao > 1:
        put_block(1, jnp.where(which(a, 1) == 0, sums[:block, block:], sums[block:, block:]))
    start = 2
    while start < ao:
        rights = green_ref[start : 2 * start].reshape(start * block, 2 * total)
        sums = lax.dot_general(left_ref[which(a, start)], rights, last, preferred_element_type=f32)
        for k in range(start, 2 * start):
            put_block(k, sums[:, (k - start) * block : (k - start + 1) * block])
        start *= 2
    at = (ao - 1) * block
    out_ref[at : at + block, :] = folded.astype(bf16)
    out_ref[at + block :, :] = jnp.broadcast_to(diagonal, (TAIL, block)).astype(bf16)


def stage_kernel(tensor_hbm, _, out_ref, tensor_ref, rows_ref, sem):
    ri_rows, block, _ = tensor_ref.shape
    a = lax.axis_index("ao")
    copy = pltpu.make_async_copy(tensor_hbm, tensor_ref, sem)
    copy.start()
    copy.wait()
    for k in range(out_ref.shape[0]):
        cols = pl.ds(pl.multiple_of((a ^ k) * block, block), block)
        for g in range(block // TILE):
            for p in range(ri_rows):
                rows_ref[p * TILE : (p + 1) * TILE, :] = tensor_ref[p, g * TILE : (g + 1) * TILE, cols]
            out_ref[k, g * block : (g + 1) * block, :] = rows_ref[...].T


def contract_kernel(count, ao, block, *refs):
    pays = refs[:count]
    tensor_ref, out_ref = refs[count:]
    ri_rows = tensor_ref.shape[2] // TILE
    a = lax.axis_index("ao")
    r = lax.axis_index("ri")
    f32, bf16 = jnp.float32, jnp.bfloat16
    groups = block // TILE
    last, plain = (((1,), (1,)), ((), ())), (((1,), (0,)), ((), ()))

    def spread(values, rows_of):
        return jnp.concatenate(
            [
                jnp.concatenate([rows_of(v, slice(g * TILE, (g + 1) * TILE)) for v in values], axis=0)
                for g in range(groups)
            ],
            axis=1,
        )

    below, on = tri_masks(block)
    at = (ao - 1) * block
    firsts, seconds = [], []
    for pay in pays:
        folded = pay[at : at + block, :].astype(f32)
        diagonal = pay[at + block : at + block + TAIL, :].astype(f32)[0:1]
        firsts.append(jnp.where(below | on, folded, 0.0).astype(bf16))
        seconds.append(
            jnp.where(below, 0.0, jnp.where(on, jnp.broadcast_to(diagonal, (block, block)), folded)).astype(bf16)
        )
    sums = lax.dot_general(
        spread(firsts + seconds, lambda v, rows: v[rows]), tensor_ref[0], plain, preferred_element_type=f32
    )
    half, width = count * TILE, ri_rows * TILE
    row = lax.broadcasted_iota(jnp.int32, (half, width), 0)
    col = lax.broadcasted_iota(jnp.int32, (half, width), 1)
    same = (row & (TILE - 1)) == (col & (TILE - 1))

    def trace(values):
        return jnp.where(same, values, 0.0).reshape(count, TILE, width).sum(axis=1)

    traces = [trace(sums[:half]), trace(sums[half:])]
    for k in range(1, ao):
        start = (k - 1) * block
        part = trace(
            lax.dot_general(
                spread(pays, lambda pay, rows: pay[start + rows.start : start + rows.stop, :]),
                tensor_ref[k],
                plain,
                preferred_element_type=f32,
            )
        )
        to_first = which(a, k) == 0
        traces[0] = traces[0] + jnp.where(to_first, part, 0.0)
        traces[1] = traces[1] + jnp.where(to_first, 0.0, part)
    traces = jnp.concatenate(traces, axis=0)
    pick = (
        lax.shift_right_logical(lax.broadcasted_iota(jnp.int32, (ri_rows, width), 1), jnp.int32(4))
        == lax.broadcasted_iota(jnp.int32, (ri_rows, width), 0)
    ).astype(f32)
    by_source = lax.dot_general(
        pick, traces, last, precision=lax.Precision.HIGHEST, preferred_element_type=f32
    )
    source = lax.broadcasted_iota(jnp.int32, (2 * count, 2 * count), 0)
    target = lax.broadcasted_iota(jnp.int32, (2 * count, 2 * count), 1)
    place = ((jnp.where(source < count, source, source - count) ^ r) * 2 + (source >= count).astype(jnp.int32)) == target
    ordered = jnp.dot(
        by_source, place.astype(f32), precision=lax.Precision.HIGHEST, preferred_element_type=f32
    )
    out_ref[...] = ordered * (1.0 / (ao * block))


def room(*arrays):
    total = sum(2 * math.prod(shape) for shape in arrays)
    return pltpu.CompilerParams(vmem_limit_bytes=min(2 * total + (4 << 20), 60 << 20))


def exchange(value, axis, size, k):
    return lax.ppermute(value, axis, [(i, i ^ k) for i in range(size)])


def along(value, targets):
    pairs = []
    for source, target in enumerate(targets):
        for core in range(2):
            other = 2 * source + 1 - core if target == source else 2 * target + core
            pairs.append((2 * source + core, other))
    return lax.ppermute(value, "ri", pairs)


def spread_along(value, ri):
    if ri != 8:
        sources = [value] + [exchange(value, "ri", ri, k) for k in range(2, ri, 2)]
        forwards = [exchange(x, "ri", ri, 1) for x in sources]
        return [x for pair in zip(sources, forwards) for x in pair]
    chip = lax.shift_right_logical(lax.axis_index("ri"), jnp.int32(1))
    inner = (chip == 1) | (chip == 2)
    middle = along(value, (0, 2, 1, 3))
    near = along(value, (1, 0, 3, 2))
    far = along(value, (3, 1, 2, 0))
    relayed, middle = lax.optimization_barrier((jnp.where(inner, middle, value), middle))
    last = along(relayed, (2, 0, 3, 1))
    across, other = jnp.where(inner, middle, far), jnp.where(inner, far, middle)
    return [value, other] + [x for y in (near, last, across) for x in (y, exchange(y, "ri", ri, 1))]


def shards(ri, ao, three_center, slab_tensor, occ_green, virt_green, pattern, atom_sizes):
    block = occ_green.shape[0]
    total = occ_green.shape[1]
    ri_rows = three_center.shape[0]
    atoms = pattern.shape[0]
    half = total + TAIL
    bf16 = jnp.bfloat16
    vmem = pl.BlockSpec(memory_space=pltpu.VMEM)
    inputs = tuple(
        pltpu.with_memory_space_constraint(x, pltpu.HBM)
        for x in (atom_sizes.reshape(1, atoms), pattern, slab_tensor, occ_green, virt_green)
    )
    size = (ao - 1) * block
    sizes = [size + (size // 2 if shared(k, ao) else size) + 2 * TAIL for k in range(1, ao)]
    prepared = pl.pallas_call(
        prep_kernel,
        out_shape=[jax.ShapeDtypeStruct((4, block, total), bf16), jax.ShapeDtypeStruct((block, total), bf16)]
        + [jax.ShapeDtypeStruct((rows, block), bf16) for rows in sizes],
        in_specs=[pl.BlockSpec(memory_space=pltpu.HBM)] * 5,
        out_specs=[vmem] * (2 + len(sizes)),
        scratch_shapes=[pltpu.VMEM(x.shape, x.dtype) for x in inputs]
        + [pltpu.VMEM((block, total), bf16), pltpu.SemaphoreType.DMA((2 + sum(len(pieces(x.shape)) for x in inputs[2:]),))],
        compiler_params=room((sum(sizes), block), (5 * block, total), (2 * block, 2 * total)),
        name="prep",
    )(*inputs)
    own, screen, *pays = prepared
    arrived = []
    for k, pay in enumerate(pays, 1):
        arrived.append(exchange(pay, "ao", ao, k))
    pays = arrived + [exchange(x, "ri", ri, 1) for k, x in enumerate(arrived, 1) if shared(k, ao)]
    groups = block // TILE
    staged = pl.pallas_call(
        stage_kernel,
        out_shape=jax.ShapeDtypeStruct((ao, groups * block, ri_rows * TILE), bf16),
        in_specs=[pl.BlockSpec(memory_space=pltpu.HBM)] * 2,
        out_specs=vmem,
        scratch_shapes=[
            pltpu.VMEM(three_center.shape, bf16),
            pltpu.VMEM((ri_rows * TILE, block), bf16),
            pltpu.SemaphoreType.DMA,
        ],
        compiler_params=room((2 * ri_rows, block, total)),
        cost_estimate=pl.CostEstimate(flops=0, transcendentals=0, bytes_accessed=8 * ri_rows * block * total),
        name="stage",
    )(pltpu.with_memory_space_constraint(three_center, pltpu.HBM), screen)
    weighted = pl.pallas_call(
        lambda *refs: transform_kernel(ao, block, *refs),
        out_shape=jax.ShapeDtypeStruct((half, block), bf16),
        in_specs=[vmem] * (len(pays) + 2) + [pl.BlockSpec(memory_space=pl.ANY)],
        out_specs=vmem,
        scratch_shapes=[
            pltpu.VMEM((2, total, total), bf16),
            pltpu.VMEM((ao, block, 2 * total), bf16),
            pltpu.VMEM((2, block, 2 * total), bf16),
        ],
        compiler_params=room((sum(sizes), block), (4 * block, total), (2, total, total), (ao, block, 2 * total), (4, block, total)),
        name="transform",
    )(*pays, own, screen, staged)
    arrived = spread_along(weighted, ri)
    part = pl.pallas_call(
        lambda *refs: contract_kernel(ri, ao, block, *refs),
        out_shape=jax.ShapeDtypeStruct((ri_rows, 2 * ri), jnp.float32),
        in_specs=[vmem] * (len(arrived) + 1),
        out_specs=vmem,
        compiler_params=room((half * len(arrived), block), (2 * ri_rows, block, total)),
        name="contract",
    )(*arrived, staged)
    parts = [part] + [exchange(part, "ao", ao, k) for k in range(1, ao)]
    while len(parts) > 1:
        parts = [parts[i] + parts[i + 1] for i in range(0, len(parts), 2)]
    return parts[0]


def solution(mesh):
    placed = (P("ri", "ao", None), P("ri", "ao", None), P("ao", None), P("ao", None), P(), P())
    ri, ao = mesh.shape["ri"], mesh.shape["ao"]

    def body(*args):
        return shards(ri, ao, *args)

    return jax.shard_map(body, mesh=mesh, in_specs=placed, out_specs=P("ri", None), check_vma=False)
```

```python
import math

import jax
import jax.numpy as jnp
from jax import lax
from jax.experimental import pallas as pl
from jax.experimental.pallas import tpu as pltpu
from jax.sharding import PartitionSpec as P


ATOM_BS = 16
TILE = 16
TAIL = 8


def top_bit(k):
    return k.bit_length() - 1


def shared(k, ao):
    return ao == 4 and k == 3


def which(a, k):
    return lax.shift_right_logical(a, jnp.int32(top_bit(k))) & 1


def tri_masks(block):
    row = lax.broadcasted_iota(jnp.int32, (block, block), 0)
    col = lax.broadcasted_iota(jnp.int32, (block, block), 1)
    return row > col, row == col


def fold_diagonal(first, second, below, on):
    folded = jnp.where(below | on, first, second)
    diagonal = jnp.sum(jnp.where(on, second, 0.0), axis=0, keepdims=True)
    return folded, diagonal


def block_at(ref, index, block):
    return ref[:, pl.ds(pl.multiple_of(index * block, block), block)]


def pieces(shape):
    half = shape[-2] // 2
    halves = [pl.ds(0, half), pl.ds(half, half)]
    return halves if len(shape) == 2 else [(i, x) for i in range(shape[0]) for x in halves]


def prep_kernel(*refs):
    hbm, mask_ref, pay_refs, copied, sems = refs[:5], refs[5], refs[6:-6], refs[-6:-1], refs[-1]
    copies = []
    for i, (src, dst) in enumerate(zip(hbm, copied)):
        parts = [(src, dst)] if i < 2 else [(src.at[x], dst.at[x]) for x in pieces(src.shape)]
        copies += [pltpu.make_async_copy(x, y, sems.at[len(copies) + n]) for n, (x, y) in enumerate(parts)]
    for copy in copies:
        copy.start()
    sizes_ref, pattern_ref, slab_ref, occ_ref, virt_ref = copied
    block = occ_ref.shape[0]
    total = occ_ref.shape[1]
    ao = total // block
    atoms = pattern_ref.shape[0]
    f32, bf16 = jnp.float32, jnp.bfloat16
    a = lax.axis_index("ao")
    row_atom = lax.shift_right_logical(
        lax.broadcasted_iota(jnp.int32, (block, atoms), 0), jnp.int32(4)
    ) + a * (block // ATOM_BS)
    pick_row = row_atom == lax.broadcasted_iota(jnp.int32, (block, atoms), 1)
    col_atom = lax.shift_right_logical(
        lax.broadcasted_iota(jnp.int32, (atoms, total), 1), jnp.int32(4)
    )
    pick_col = (col_atom == lax.broadcasted_iota(jnp.int32, (atoms, total), 0)).astype(f32).astype(bf16)
    copies[0].wait()
    copies[1].wait()
    sizes = sizes_ref[...].astype(f32)
    size_row = jnp.sum(jnp.where(pick_row, jnp.broadcast_to(sizes, (block, atoms)), 0.0), axis=1, keepdims=True)
    size_col = jnp.dot(
        jnp.broadcast_to(sizes, (8, atoms)).astype(bf16), pick_col, preferred_element_type=f32
    )[0:1]
    rows = jnp.dot(
        pick_row.astype(f32).astype(bf16), pattern_ref[...].astype(f32).astype(bf16),
        preferred_element_type=f32,
    ).astype(bf16)
    kept = jnp.dot(rows, pick_col, preferred_element_type=f32)
    slot_row = (lax.broadcasted_iota(jnp.int32, (block, total), 0) & (ATOM_BS - 1)).astype(f32)
    slot_col = (lax.broadcasted_iota(jnp.int32, (block, total), 1) & (ATOM_BS - 1)).astype(f32)
    live = (slot_row < size_row) & (slot_col < size_col)
    mask_ref[...] = jnp.where(live, kept, 0.0).astype(bf16)
    below, on = tri_masks(block)
    for copy in copies[2:]:
        copy.wait()
    even = (lax.axis_index("ri") & 1) == 0
    rows, size = block // 2, (ao - 1) * block

    def put(place, k, whole):
        for m in range(1, ao):
            if m == k:
                continue
            value, step = whole, block
            if place == 1 and shared(m, ao):
                value, step = jnp.where(even, whole[:rows], whole[rows:]), rows
            at = place * size + ((ao - 2) if k == 0 else k - 1 - (k > m)) * step
            pay_refs[m - 1][at : at + step, :] = value

    tails = []
    for k in range(1, ao + 1):
        k %= ao
        screen = block_at(mask_ref, a ^ k, block)
        cols = pl.ds(pl.multiple_of((a ^ k) * block, block), block)
        for place in range(2):
            if place == 0:
                pair = [slab_ref[q, :, cols] * screen for q in range(2)]
            else:
                pair = [occ_ref[:, cols], virt_ref[:, cols]]
            if k:
                value = jnp.where(which(a, k) == 0, *pair)
            else:
                value, diagonal = fold_diagonal(*(x.astype(f32) for x in pair), below, on)
                value = value.astype(bf16)
                tails.append(diagonal)
            put(place, k, value)
    upper = lax.broadcasted_iota(jnp.int32, (2 * TAIL, block), 0) < TAIL
    tail = jnp.where(upper, *tails).astype(bf16)
    for ref in pay_refs:
        ref[ref.shape[0] - 2 * TAIL :, :] = tail


def reader(ref, base, m, ao, block):
    def read(k):
        at = base + ((ao - 2) if k == 0 else k - 1 - (k > m)) * block
        return ref[at : at + block, :]

    return read


def halves_reader(mine, other, even, base, m, ao, block):
    here, there = (reader(x, base, m, ao, block // 2) for x in (mine, other))

    def read(k):
        x, y = here(k), there(k)
        return jnp.concatenate([jnp.where(even, x, y), jnp.where(even, y, x)], axis=0)

    return read


def unfold(reads, diagonals, own, a, ao, block, put):
    below, on = tri_masks(block)
    for q in range(2):
        for k in range(ao):
            value = own(q, k)
            put(q, 0, k, value)
            if k:
                put(q, k, 0, value.T)
    for m in range(1, ao):
        for k in range(1, ao):
            if k != m:
                value = reads[m](k)
                put(which(a ^ m, k), m, m ^ k, value)
                put(which(a ^ m, k), m ^ k, m, value.T)
        folded = reads[m](0).astype(jnp.float32)
        folded_t = folded.T
        diagonal = diagonals[m]
        put(0, m, m, jnp.where(below | on, folded, folded_t).astype(jnp.bfloat16))
        put(
            1, m, m,
            jnp.where(below, folded_t, jnp.where(on, jnp.broadcast_to(diagonal, (block, block)), folded)).astype(
                jnp.bfloat16
            ),
        )


def transform_kernel(ao, block, *refs):
    own_ref, screen_ref, _, out_ref, slab_ref, green_ref, left_ref = refs[-7:]
    pays = refs[:-7]
    total = ao * block
    a = lax.axis_index("ao")
    f32, bf16 = jnp.float32, jnp.bfloat16
    size = (ao - 1) * block
    pays, others = pays[: ao - 1], list(pays[ao - 1 :])
    even = (lax.axis_index("ri") & 1) == 0
    slabs, greens, diagonals = [None], [None], ([None], [None])
    for m, x in enumerate(pays, 1):
        tail = x[x.shape[0] - 2 * TAIL :, :].astype(f32)
        for rows, at in zip(diagonals, (0, TAIL)):
            rows.append(tail[at : at + 1])
        slabs.append(reader(x, 0, m, ao, block))
        if shared(m, ao):
            greens.append(halves_reader(x, others.pop(0), even, size, m, ao, block))
        else:
            greens.append(reader(x, size, m, ao, block))

    def put_slab(matrix, row, col, value):
        slab_ref[matrix, row * block : (row + 1) * block, col * block : (col + 1) * block] = value

    def put_green(matrix, row, col, value):
        at = pl.multiple_of((1 - matrix) * total + col * block, block)
        green_ref[row, :, pl.ds(at, block)] = value

    def own(first):
        return lambda q, k: own_ref[first + q, :, k * block : (k + 1) * block]

    unfold(slabs, diagonals[0], own(0), a, ao, block, put_slab)
    both = own_ref[2:4].reshape(2 * block, total)
    for q in range(2):
        left = jnp.dot(both, slab_ref[q], preferred_element_type=f32).astype(bf16)
        left_ref[q, :, :total] = left[:block]
        left_ref[q, :, total:] = left[block:]
    unfold(greens, diagonals[1], own(2), a, ao, block, put_green)
    last = (((1,), (1,)), ((), ()))
    below, on = tri_masks(block)

    def put_block(k, sums):
        screen = screen_ref[:, k * block : (k + 1) * block].astype(f32)
        out_ref[(k - 1) * block : k * block, :] = (sums * screen).astype(bf16)

    lefts = jnp.concatenate([left_ref[0], left_ref[1]], axis=0)
    rights = green_ref[0 : min(2, ao)].reshape(min(2, ao) * block, 2 * total)
    sums = lax.dot_general(lefts, rights, last, preferred_element_type=f32)
    weight = jnp.where(on, 0.5, 1.0) * screen_ref[:, 0:block].astype(f32)
    folded, diagonal = fold_diagonal(sums[:block, :block] * weight, sums[block:, :block] * weight, below, on)
    if ao > 1:
        put_block(1, jnp.where(which(a, 1) == 0, sums[:block, block:], sums[block:, block:]))
    start = 2
    while start < ao:
        rights = green_ref[start : 2 * start].reshape(start * block, 2 * total)
        sums = lax.dot_general(left_ref[which(a, start)], rights, last, preferred_element_type=f32)
        for k in range(start, 2 * start):
            put_block(k, sums[:, (k - start) * block : (k - start + 1) * block])
        start *= 2
    at = (ao - 1) * block
    out_ref[at : at + block, :] = folded.astype(bf16)
    out_ref[at + block :, :] = jnp.broadcast_to(diagonal, (TAIL, block)).astype(bf16)


def stage_kernel(tensor_hbm, slab_hbm, occ_hbm, virt_hbm, mask_ref, out_ref, own_ref, screen_ref, *scratch):
    tensor_ref, slab_ref, occ_ref, virt_ref, rows_ref, sems = scratch
    ri_rows, block, _ = tensor_ref.shape
    a = lax.axis_index("ao")
    sources = (slab_hbm, occ_hbm, virt_hbm, tensor_hbm)
    targets = (slab_ref, occ_ref, virt_ref, tensor_ref)
    copies = [pltpu.make_async_copy(x, y, sems.at[i]) for i, (x, y) in enumerate(zip(sources, targets))]
    for copy in copies:
        copy.start()
    for copy in copies[:3]:
        copy.wait()
    for k in range(out_ref.shape[0]):
        cols = pl.ds(pl.multiple_of((a ^ k) * block, block), block)
        span = slice(k * block, (k + 1) * block)
        screen = mask_ref[:, cols]
        screen_ref[:, span] = screen
        for q in range(2):
            own_ref[q, :, span] = slab_ref[q, :, cols] * screen
        own_ref[2, :, span] = occ_ref[:, cols]
        own_ref[3, :, span] = virt_ref[:, cols]
    copies[3].wait()
    for k in range(out_ref.shape[0]):
        cols = pl.ds(pl.multiple_of((a ^ k) * block, block), block)
        for g in range(block // TILE):
            for p in range(ri_rows):
                rows_ref[p * TILE : (p + 1) * TILE, :] = tensor_ref[p, g * TILE : (g + 1) * TILE, cols]
            out_ref[k, g * block : (g + 1) * block, :] = rows_ref[...].T


def contract_kernel(count, ao, block, *refs):
    pays = refs[:count]
    tensor_ref, out_ref = refs[count:]
    ri_rows = tensor_ref.shape[2] // TILE
    a = lax.axis_index("ao")
    r = lax.axis_index("ri")
    f32, bf16 = jnp.float32, jnp.bfloat16
    groups = block // TILE
    last, plain = (((1,), (1,)), ((), ())), (((1,), (0,)), ((), ()))

    def spread(values, rows_of):
        return jnp.concatenate(
            [
                jnp.concatenate([rows_of(v, slice(g * TILE, (g + 1) * TILE)) for v in values], axis=0)
                for g in range(groups)
            ],
            axis=1,
        )

    below, on = tri_masks(block)
    at = (ao - 1) * block
    firsts, seconds = [], []
    for pay in pays:
        folded = pay[at : at + block, :].astype(f32)
        diagonal = pay[at + block : at + block + TAIL, :].astype(f32)[0:1]
        firsts.append(jnp.where(below | on, folded, 0.0).astype(bf16))
        seconds.append(
            jnp.where(below, 0.0, jnp.where(on, jnp.broadcast_to(diagonal, (block, block)), folded)).astype(bf16)
        )
    sums = lax.dot_general(
        spread(firsts + seconds, lambda v, rows: v[rows]), tensor_ref[0], plain, preferred_element_type=f32
    )
    half, width = count * TILE, ri_rows * TILE
    row = lax.broadcasted_iota(jnp.int32, (half, width), 0)
    col = lax.broadcasted_iota(jnp.int32, (half, width), 1)
    same = (row & (TILE - 1)) == (col & (TILE - 1))

    def trace(values):
        return jnp.where(same, values, 0.0).reshape(count, TILE, width).sum(axis=1)

    traces = [trace(sums[:half]), trace(sums[half:])]
    first = max(1, ao // 2)
    while first >= 1 and ao > 1:
        lefts = [
            spread(pays, lambda pay, rows, at=(k - 1) * block: pay[at + rows.start : at + rows.stop, :])
            for k in range(first, 2 * first)
        ]
        rights = tensor_ref[first : 2 * first].reshape(first * groups * block, width)
        part = trace(
            lax.dot_general(jnp.concatenate(lefts, axis=1), rights, plain, preferred_element_type=f32)
        )
        to_first = which(a, first) == 0
        traces[0] = traces[0] + jnp.where(to_first, part, 0.0)
        traces[1] = traces[1] + jnp.where(to_first, 0.0, part)
        first //= 2
    traces = jnp.concatenate(traces, axis=0)
    pick = (
        lax.shift_right_logical(lax.broadcasted_iota(jnp.int32, (ri_rows, width), 1), jnp.int32(4))
        == lax.broadcasted_iota(jnp.int32, (ri_rows, width), 0)
    ).astype(f32)
    by_source = lax.dot_general(
        pick, traces, last, precision=lax.Precision.HIGHEST, preferred_element_type=f32
    )
    source = lax.broadcasted_iota(jnp.int32, (2 * count, 2 * count), 0)
    target = lax.broadcasted_iota(jnp.int32, (2 * count, 2 * count), 1)
    place = ((jnp.where(source < count, source, source - count) ^ r) * 2 + (source >= count).astype(jnp.int32)) == target
    ordered = jnp.dot(
        by_source, place.astype(f32), precision=lax.Precision.HIGHEST, preferred_element_type=f32
    )
    out_ref[...] = ordered * (1.0 / (ao * block))


def room(*arrays):
    total = sum(2 * math.prod(shape) for shape in arrays)
    return pltpu.CompilerParams(vmem_limit_bytes=min(2 * total + (4 << 20), 60 << 20))


def exchange(value, axis, size, k):
    return lax.ppermute(value, axis, [(i, i ^ k) for i in range(size)])


def along(value, targets):
    pairs = []
    for source, target in enumerate(targets):
        for core in range(2):
            other = 2 * source + 1 - core if target == source else 2 * target + core
            pairs.append((2 * source + core, other))
    return lax.ppermute(value, "ri", pairs)


def spread_along(value, ri):
    if ri != 8:
        sources = [value] + [exchange(value, "ri", ri, k) for k in range(2, ri, 2)]
        forwards = [exchange(x, "ri", ri, 1) for x in sources]
        return [x for pair in zip(sources, forwards) for x in pair]
    chip = lax.shift_right_logical(lax.axis_index("ri"), jnp.int32(1))
    inner = (chip == 1) | (chip == 2)
    middle = along(value, (0, 2, 1, 3))
    near = along(value, (1, 0, 3, 2))
    far = along(value, (3, 1, 2, 0))
    relayed, middle = lax.optimization_barrier((jnp.where(inner, middle, value), middle))
    last = along(relayed, (2, 0, 3, 1))
    across, other = jnp.where(inner, middle, far), jnp.where(inner, far, middle)
    return [value, other] + [x for y in (near, last, across) for x in (y, exchange(y, "ri", ri, 1))]


def shards(ri, ao, three_center, slab_tensor, occ_green, virt_green, pattern, atom_sizes):
    block = occ_green.shape[0]
    total = occ_green.shape[1]
    ri_rows = three_center.shape[0]
    atoms = pattern.shape[0]
    half = total + TAIL
    bf16 = jnp.bfloat16
    vmem = pl.BlockSpec(memory_space=pltpu.VMEM)
    inputs = tuple(
        pltpu.with_memory_space_constraint(x, pltpu.HBM)
        for x in (atom_sizes.reshape(1, atoms), pattern, slab_tensor, occ_green, virt_green)
    )
    size = (ao - 1) * block
    sizes = [size + (size // 2 if shared(k, ao) else size) + 2 * TAIL for k in range(1, ao)]
    prepared = pl.pallas_call(
        prep_kernel,
        out_shape=[jax.ShapeDtypeStruct((block, total), bf16)]
        + [jax.ShapeDtypeStruct((rows, block), bf16) for rows in sizes],
        in_specs=[pl.BlockSpec(memory_space=pltpu.HBM)] * 5,
        out_specs=[vmem] * (1 + len(sizes)),
        scratch_shapes=[pltpu.VMEM(x.shape, x.dtype) for x in inputs]
        + [pltpu.SemaphoreType.DMA((2 + sum(len(pieces(x.shape)) for x in inputs[2:]),))],
        compiler_params=room((sum(sizes), block), (5 * block, total), (2 * block, 2 * total)),
        name="prep",
    )(*inputs)
    mask, *pays = prepared
    arrived = []
    for k, pay in enumerate(pays, 1):
        arrived.append(exchange(pay, "ao", ao, k))
    pays = arrived + [exchange(x, "ri", ri, 1) for k, x in enumerate(arrived, 1) if shared(k, ao)]
    groups = block // TILE
    rows = ri_rows * TILE
    staged, own, screen = pl.pallas_call(
        stage_kernel,
        out_shape=[
            jax.ShapeDtypeStruct((ao, groups * block, rows), bf16),
            jax.ShapeDtypeStruct((4, block, total), bf16),
            jax.ShapeDtypeStruct((block, total), bf16),
        ],
        in_specs=[pl.BlockSpec(memory_space=pltpu.HBM)] * 4 + [vmem],
        out_specs=[vmem] * 3,
        scratch_shapes=[pltpu.VMEM(x.shape, bf16) for x in (three_center, *inputs[2:])]
        + [pltpu.VMEM((rows, block), bf16), pltpu.SemaphoreType.DMA((4,))],
        compiler_params=room((2 * ri_rows, block, total), (8 * block, total)),
        cost_estimate=pl.CostEstimate(flops=0, transcendentals=0, bytes_accessed=8 * ri_rows * block * total),
        name="stage",
    )(pltpu.with_memory_space_constraint(three_center, pltpu.HBM), *inputs[2:], mask)
    weighted = pl.pallas_call(
        lambda *refs: transform_kernel(ao, block, *refs),
        out_shape=jax.ShapeDtypeStruct((half, block), bf16),
        in_specs=[vmem] * (len(pays) + 2) + [pl.BlockSpec(memory_space=pl.ANY)],
        out_specs=vmem,
        scratch_shapes=[
            pltpu.VMEM((2, total, total), bf16),
            pltpu.VMEM((ao, block, 2 * total), bf16),
            pltpu.VMEM((2, block, 2 * total), bf16),
        ],
        compiler_params=room((sum(sizes), block), (4 * block, total), (2, total, total), (ao, block, 2 * total), (4, block, total)),
        name="transform",
    )(*pays, own, screen, staged)
    arrived = spread_along(weighted, ri)
    part = pl.pallas_call(
        lambda *refs: contract_kernel(ri, ao, block, *refs),
        out_shape=jax.ShapeDtypeStruct((ri_rows, 2 * ri), jnp.float32),
        in_specs=[vmem] * (len(arrived) + 1),
        out_specs=vmem,
        compiler_params=room((half * len(arrived), block), (2 * ri_rows, block, total)),
        name="contract",
    )(*arrived, staged)
    parts = [part] + [exchange(part, "ao", ao, k) for k in range(1, ao)]
    while len(parts) > 1:
        parts = [parts[i] + parts[i + 1] for i in range(0, len(parts), 2)]
    return parts[0]


def solution(mesh):
    placed = (P("ri", "ao", None), P("ri", "ao", None), P("ao", None), P("ao", None), P(), P())
    ri, ao = mesh.shape["ri"], mesh.shape["ao"]

    def body(*args):
        return shards(ri, ao, *args)

    return jax.shard_map(body, mesh=mesh, in_specs=placed, out_specs=P("ri", None), check_vma=False)
```

```python
import math

import jax
import jax.numpy as jnp
from jax import lax
from jax.experimental import pallas as pl
from jax.experimental.pallas import tpu as pltpu
from jax.sharding import PartitionSpec as P


ATOM_BS = 16
TILE = 16
TAIL = 8


def top_bit(k):
    return k.bit_length() - 1


def shared(k, ao):
    return ao == 4 and k == 3


def which(a, k):
    return lax.shift_right_logical(a, jnp.int32(top_bit(k))) & 1


def tri_masks(block):
    row = lax.broadcasted_iota(jnp.int32, (block, block), 0)
    col = lax.broadcasted_iota(jnp.int32, (block, block), 1)
    return row > col, row == col


def fold_diagonal(first, second, below, on):
    folded = jnp.where(below | on, first, second)
    diagonal = jnp.sum(jnp.where(on, second, 0.0), axis=0, keepdims=True)
    return folded, diagonal


def block_at(ref, index, block):
    return ref[:, pl.ds(pl.multiple_of(index * block, block), block)]


def prep_kernel(*refs):
    hbm, mask_ref, pay_refs, copied, sems = refs[:5], refs[5], refs[6:-6], refs[-6:-1], refs[-1]
    copies = []
    for i, (src, dst) in enumerate(zip(hbm, copied)):
        copies.append(pltpu.make_async_copy(src, dst, sems.at[i]))
    for copy in copies:
        copy.start()
    sizes_ref, pattern_ref, slab_ref, occ_ref, virt_ref = copied
    block = occ_ref.shape[0]
    total = occ_ref.shape[1]
    ao = total // block
    atoms = pattern_ref.shape[0]
    f32, bf16 = jnp.float32, jnp.bfloat16
    a = lax.axis_index("ao")
    row_atom = lax.shift_right_logical(
        lax.broadcasted_iota(jnp.int32, (block, atoms), 0), jnp.int32(4)
    ) + a * (block // ATOM_BS)
    pick_row = row_atom == lax.broadcasted_iota(jnp.int32, (block, atoms), 1)
    col_atom = lax.shift_right_logical(
        lax.broadcasted_iota(jnp.int32, (atoms, total), 1), jnp.int32(4)
    )
    pick_col = (col_atom == lax.broadcasted_iota(jnp.int32, (atoms, total), 0)).astype(f32).astype(bf16)
    copies[0].wait()
    copies[1].wait()
    sizes = sizes_ref[...].astype(f32)
    size_row = jnp.sum(jnp.where(pick_row, jnp.broadcast_to(sizes, (block, atoms)), 0.0), axis=1, keepdims=True)
    size_col = jnp.dot(
        jnp.broadcast_to(sizes, (8, atoms)).astype(bf16), pick_col, preferred_element_type=f32
    )[0:1]
    rows = jnp.dot(
        pick_row.astype(f32).astype(bf16), pattern_ref[...].astype(f32).astype(bf16),
        preferred_element_type=f32,
    ).astype(bf16)
    kept = jnp.dot(rows, pick_col, preferred_element_type=f32)
    slot_row = (lax.broadcasted_iota(jnp.int32, (block, total), 0) & (ATOM_BS - 1)).astype(f32)
    slot_col = (lax.broadcasted_iota(jnp.int32, (block, total), 1) & (ATOM_BS - 1)).astype(f32)
    live = (slot_row < size_row) & (slot_col < size_col)
    mask_ref[...] = jnp.where(live, kept, 0.0).astype(bf16)
    below, on = tri_masks(block)
    for copy in copies[2:]:
        copy.wait()
    even = (lax.axis_index("ri") & 1) == 0
    rows, size = block // 2, (ao - 1) * block

    def put(place, k, whole):
        for m in range(1, ao):
            if m == k:
                continue
            value, step = whole, block
            if place == 1 and shared(m, ao):
                value, step = jnp.where(even, whole[:rows], whole[rows:]), rows
            at = place * size + ((ao - 2) if k == 0 else k - 1 - (k > m)) * step
            pay_refs[m - 1][at : at + step, :] = value

    tails = []
    for k in range(1, ao + 1):
        k %= ao
        screen = block_at(mask_ref, a ^ k, block)
        cols = pl.ds(pl.multiple_of((a ^ k) * block, block), block)
        for place in range(2):
            if place == 0:
                pair = [slab_ref[q, :, cols] * screen for q in range(2)]
            else:
                pair = [occ_ref[:, cols], virt_ref[:, cols]]
            if k:
                value = jnp.where(which(a, k) == 0, *pair)
            else:
                value, diagonal = fold_diagonal(*(x.astype(f32) for x in pair), below, on)
                value = value.astype(bf16)
                tails.append(diagonal)
            put(place, k, value)
    upper = lax.broadcasted_iota(jnp.int32, (2 * TAIL, block), 0) < TAIL
    tail = jnp.where(upper, *tails).astype(bf16)
    for ref in pay_refs:
        ref[ref.shape[0] - 2 * TAIL :, :] = tail


def reader(ref, base, m, ao, block):
    def read(k):
        at = base + ((ao - 2) if k == 0 else k - 1 - (k > m)) * block
        return ref[at : at + block, :]

    return read


def halves_reader(mine, other, even, base, m, ao, block):
    here, there = (reader(x, base, m, ao, block // 2) for x in (mine, other))

    def read(k):
        x, y = here(k), there(k)
        return jnp.concatenate([jnp.where(even, x, y), jnp.where(even, y, x)], axis=0)

    return read


def unfold(reads, diagonals, own, a, ao, block, put):
    below, on = tri_masks(block)
    for q in range(2):
        for k in range(ao):
            value = own(q, k)
            put(q, 0, k, value)
            if k:
                put(q, k, 0, value.T)
    for m in range(1, ao):
        for k in range(1, ao):
            if k != m:
                value = reads[m](k)
                put(which(a ^ m, k), m, m ^ k, value)
                put(which(a ^ m, k), m ^ k, m, value.T)
        folded = reads[m](0).astype(jnp.float32)
        folded_t = folded.T
        diagonal = diagonals[m]
        put(0, m, m, jnp.where(below | on, folded, folded_t).astype(jnp.bfloat16))
        put(
            1, m, m,
            jnp.where(below, folded_t, jnp.where(on, jnp.broadcast_to(diagonal, (block, block)), folded)).astype(
                jnp.bfloat16
            ),
        )


def transform_kernel(ao, block, *refs):
    own_ref, screen_ref, _, out_ref, slab_ref, green_ref, left_ref = refs[-7:]
    pays = refs[:-7]
    total = ao * block
    a = lax.axis_index("ao")
    f32, bf16 = jnp.float32, jnp.bfloat16
    size = (ao - 1) * block
    pays, others = pays[: ao - 1], list(pays[ao - 1 :])
    even = (lax.axis_index("ri") & 1) == 0
    slabs, greens, diagonals = [None], [None], ([None], [None])
    for m, x in enumerate(pays, 1):
        tail = x[x.shape[0] - 2 * TAIL :, :].astype(f32)
        for rows, at in zip(diagonals, (0, TAIL)):
            rows.append(tail[at : at + 1])
        slabs.append(reader(x, 0, m, ao, block))
        if shared(m, ao):
            greens.append(halves_reader(x, others.pop(0), even, size, m, ao, block))
        else:
            greens.append(reader(x, size, m, ao, block))

    def put_slab(matrix, row, col, value):
        slab_ref[matrix, row * block : (row + 1) * block, col * block : (col + 1) * block] = value

    def put_green(matrix, row, col, value):
        at = pl.multiple_of((1 - matrix) * total + col * block, block)
        green_ref[row, :, pl.ds(at, block)] = value

    def own(first):
        return lambda q, k: own_ref[first + q, :, k * block : (k + 1) * block]

    unfold(slabs, diagonals[0], own(0), a, ao, block, put_slab)
    both = own_ref[2:4].reshape(2 * block, total)
    for q in range(2):
        left = jnp.dot(both, slab_ref[q], preferred_element_type=f32).astype(bf16)
        left_ref[q, :, :total] = left[:block]
        left_ref[q, :, total:] = left[block:]
    unfold(greens, diagonals[1], own(2), a, ao, block, put_green)
    last = (((1,), (1,)), ((), ()))
    below, on = tri_masks(block)

    def put_block(k, sums):
        screen = screen_ref[:, k * block : (k + 1) * block].astype(f32)
        out_ref[(k - 1) * block : k * block, :] = (sums * screen).astype(bf16)

    lefts = jnp.concatenate([left_ref[0], left_ref[1]], axis=0)
    rights = green_ref[0 : min(2, ao)].reshape(min(2, ao) * block, 2 * total)
    sums = lax.dot_general(lefts, rights, last, preferred_element_type=f32)
    weight = jnp.where(on, 0.5, 1.0) * screen_ref[:, 0:block].astype(f32)
    folded, diagonal = fold_diagonal(sums[:block, :block] * weight, sums[block:, :block] * weight, below, on)
    if ao > 1:
        put_block(1, jnp.where(which(a, 1) == 0, sums[:block, block:], sums[block:, block:]))
    start = 2
    while start < ao:
        rights = green_ref[start : 2 * start].reshape(start * block, 2 * total)
        sums = lax.dot_general(left_ref[which(a, start)], rights, last, preferred_element_type=f32)
        for k in range(start, 2 * start):
            put_block(k, sums[:, (k - start) * block : (k - start + 1) * block])
        start *= 2
    at = (ao - 1) * block
    out_ref[at : at + block, :] = folded.astype(bf16)
    out_ref[at + block :, :] = jnp.broadcast_to(diagonal, (TAIL, block)).astype(bf16)


def stage_kernel(tensor_hbm, slab_hbm, occ_hbm, virt_hbm, mask_ref, out_ref, own_ref, screen_ref, *scratch):
    tensor_ref, slab_ref, occ_ref, virt_ref, rows_ref, sems = scratch
    ri_rows, block, _ = tensor_ref.shape
    a = lax.axis_index("ao")
    sources = (slab_hbm, occ_hbm, virt_hbm, tensor_hbm)
    targets = (slab_ref, occ_ref, virt_ref, tensor_ref)
    copies = [pltpu.make_async_copy(x, y, sems.at[i]) for i, (x, y) in enumerate(zip(sources, targets))]
    for copy in copies:
        copy.start()
    for copy in copies[:3]:
        copy.wait()
    for k in range(out_ref.shape[0]):
        cols = pl.ds(pl.multiple_of((a ^ k) * block, block), block)
        span = slice(k * block, (k + 1) * block)
        screen = mask_ref[:, cols]
        screen_ref[:, span] = screen
        for q in range(2):
            own_ref[q, :, span] = slab_ref[q, :, cols] * screen
        own_ref[2, :, span] = occ_ref[:, cols]
        own_ref[3, :, span] = virt_ref[:, cols]
    copies[3].wait()
    for k in range(out_ref.shape[0]):
        cols = pl.ds(pl.multiple_of((a ^ k) * block, block), block)
        for g in range(block // TILE):
            for p in range(ri_rows):
                rows_ref[p * TILE : (p + 1) * TILE, :] = tensor_ref[p, g * TILE : (g + 1) * TILE, cols]
            out_ref[k, g * block : (g + 1) * block, :] = rows_ref[...].T


def contract_kernel(count, ao, block, *refs):
    pays = refs[:count]
    tensor_ref, out_ref = refs[count:]
    ri_rows = tensor_ref.shape[2] // TILE
    a = lax.axis_index("ao")
    r = lax.axis_index("ri")
    f32, bf16 = jnp.float32, jnp.bfloat16
    groups = block // TILE
    last, plain = (((1,), (1,)), ((), ())), (((1,), (0,)), ((), ()))

    def spread(values, rows_of):
        return jnp.concatenate(
            [
                jnp.concatenate([rows_of(v, slice(g * TILE, (g + 1) * TILE)) for v in values], axis=0)
                for g in range(groups)
            ],
            axis=1,
        )

    below, on = tri_masks(block)
    at = (ao - 1) * block
    firsts, seconds = [], []
    for pay in pays:
        folded = pay[at : at + block, :].astype(f32)
        diagonal = pay[at + block : at + block + TAIL, :].astype(f32)[0:1]
        firsts.append(jnp.where(below | on, folded, 0.0).astype(bf16))
        seconds.append(
            jnp.where(below, 0.0, jnp.where(on, jnp.broadcast_to(diagonal, (block, block)), folded)).astype(bf16)
        )
    sums = lax.dot_general(
        spread(firsts + seconds, lambda v, rows: v[rows]), tensor_ref[0], plain, preferred_element_type=f32
    )
    half, width = count * TILE, ri_rows * TILE
    row = lax.broadcasted_iota(jnp.int32, (half, width), 0)
    col = lax.broadcasted_iota(jnp.int32, (half, width), 1)
    same = (row & (TILE - 1)) == (col & (TILE - 1))

    def trace(values):
        return jnp.where(same, values, 0.0).reshape(count, TILE, width).sum(axis=1)

    traces = [trace(sums[:half]), trace(sums[half:])]
    first = max(1, ao // 2)
    while first >= 1 and ao > 1:
        lefts = [
            spread(pays, lambda pay, rows, at=(k - 1) * block: pay[at + rows.start : at + rows.stop, :])
            for k in range(first, 2 * first)
        ]
        rights = tensor_ref[first : 2 * first].reshape(first * groups * block, width)
        part = trace(
            lax.dot_general(jnp.concatenate(lefts, axis=1), rights, plain, preferred_element_type=f32)
        )
        to_first = which(a, first) == 0
        traces[0] = traces[0] + jnp.where(to_first, part, 0.0)
        traces[1] = traces[1] + jnp.where(to_first, 0.0, part)
        first //= 2
    traces = jnp.concatenate(traces, axis=0)

    def parts(values):
        out, rest = [], values
        for _ in range(3):
            out.append(rest.astype(bf16))
            rest = rest - out[-1].astype(f32)
        return jnp.concatenate(out, axis=0)

    wide = 3 * 2 * count
    target = lax.broadcasted_iota(jnp.int32, (2 * count, wide), 0)
    source = lax.broadcasted_iota(jnp.int32, (2 * count, wide), 1)
    source = jnp.where(source >= 4 * count, source - 4 * count, source)
    source = jnp.where(source >= 2 * count, source - 2 * count, source)
    second = source >= count
    place = ((jnp.where(second, source - count, source) ^ r) * 2 + second.astype(jnp.int32)) == target
    placed = jnp.dot(place.astype(f32).astype(bf16), parts(traces), preferred_element_type=f32)
    pick = (
        lax.shift_right_logical(lax.broadcasted_iota(jnp.int32, (ri_rows, width), 1), jnp.int32(4))
        == lax.broadcasted_iota(jnp.int32, (ri_rows, width), 0)
    ).astype(f32).astype(bf16)
    split = parts(placed)
    ordered = sum(
        lax.dot_general(
            pick, split[n * 2 * count : (n + 1) * 2 * count], last, preferred_element_type=f32
        )
        for n in range(3)
    )
    out_ref[...] = ordered * (1.0 / (ao * block))


def room(*arrays):
    total = sum(2 * math.prod(shape) for shape in arrays)
    return pltpu.CompilerParams(vmem_limit_bytes=min(2 * total + (4 << 20), 60 << 20))


def exchange(value, axis, size, k):
    return lax.ppermute(value, axis, [(i, i ^ k) for i in range(size)])


def along(value, targets):
    pairs = []
    for source, target in enumerate(targets):
        for core in range(2):
            other = 2 * source + 1 - core if target == source else 2 * target + core
            pairs.append((2 * source + core, other))
    return lax.ppermute(value, "ri", pairs)


def spread_along(value, ri):
    if ri != 8:
        sources = [value] + [exchange(value, "ri", ri, k) for k in range(2, ri, 2)]
        forwards = [exchange(x, "ri", ri, 1) for x in sources]
        return [x for pair in zip(sources, forwards) for x in pair]
    chip = lax.shift_right_logical(lax.axis_index("ri"), jnp.int32(1))
    inner = (chip == 1) | (chip == 2)
    middle = along(value, (0, 2, 1, 3))
    near = along(value, (1, 0, 3, 2))
    far = along(value, (3, 1, 2, 0))
    relayed, middle = lax.optimization_barrier((jnp.where(inner, middle, value), middle))
    last = along(relayed, (2, 0, 3, 1))
    across, other = jnp.where(inner, middle, far), jnp.where(inner, far, middle)
    return [value, other] + [x for y in (near, last, across) for x in (y, exchange(y, "ri", ri, 1))]


def shards(ri, ao, three_center, slab_tensor, occ_green, virt_green, pattern, atom_sizes):
    block = occ_green.shape[0]
    total = occ_green.shape[1]
    ri_rows = three_center.shape[0]
    atoms = pattern.shape[0]
    half = total + TAIL
    bf16 = jnp.bfloat16
    vmem = pl.BlockSpec(memory_space=pltpu.VMEM)
    inputs = tuple(
        pltpu.with_memory_space_constraint(x, pltpu.HBM)
        for x in (atom_sizes.reshape(1, atoms), pattern, slab_tensor, occ_green, virt_green)
    )
    size = (ao - 1) * block
    sizes = [size + (size // 2 if shared(k, ao) else size) + 2 * TAIL for k in range(1, ao)]
    prepared = pl.pallas_call(
        prep_kernel,
        out_shape=[jax.ShapeDtypeStruct((block, total), bf16)]
        + [jax.ShapeDtypeStruct((rows, block), bf16) for rows in sizes],
        in_specs=[pl.BlockSpec(memory_space=pltpu.HBM)] * 5,
        out_specs=[vmem] * (1 + len(sizes)),
        scratch_shapes=[pltpu.VMEM(x.shape, x.dtype) for x in inputs]
        + [pltpu.SemaphoreType.DMA((len(inputs),))],
        compiler_params=room((sum(sizes), block), (5 * block, total), (2 * block, 2 * total)),
        name="prep",
    )(*inputs)
    mask, *pays = prepared
    arrived = []
    for k, pay in enumerate(pays, 1):
        arrived.append(exchange(pay, "ao", ao, k))
    pays = arrived + [exchange(x, "ri", ri, 1) for k, x in enumerate(arrived, 1) if shared(k, ao)]
    groups = block // TILE
    rows = ri_rows * TILE
    staged, own, screen = pl.pallas_call(
        stage_kernel,
        out_shape=[
            jax.ShapeDtypeStruct((ao, groups * block, rows), bf16),
            jax.ShapeDtypeStruct((4, block, total), bf16),
            jax.ShapeDtypeStruct((block, total), bf16),
        ],
        in_specs=[pl.BlockSpec(memory_space=pltpu.HBM)] * 4 + [vmem],
        out_specs=[vmem] * 3,
        scratch_shapes=[pltpu.VMEM(x.shape, bf16) for x in (three_center, *inputs[2:])]
        + [pltpu.VMEM((rows, block), bf16), pltpu.SemaphoreType.DMA((4,))],
        compiler_params=room((2 * ri_rows, block, total), (8 * block, total)),
        cost_estimate=pl.CostEstimate(flops=0, transcendentals=0, bytes_accessed=8 * ri_rows * block * total),
        name="stage",
    )(pltpu.with_memory_space_constraint(three_center, pltpu.HBM), *inputs[2:], mask)
    weighted = pl.pallas_call(
        lambda *refs: transform_kernel(ao, block, *refs),
        out_shape=jax.ShapeDtypeStruct((half, block), bf16),
        in_specs=[vmem] * (len(pays) + 2) + [pl.BlockSpec(memory_space=pl.ANY)],
        out_specs=vmem,
        scratch_shapes=[
            pltpu.VMEM((2, total, total), bf16),
            pltpu.VMEM((ao, block, 2 * total), bf16),
            pltpu.VMEM((2, block, 2 * total), bf16),
        ],
        compiler_params=room((sum(sizes), block), (4 * block, total), (2, total, total), (ao, block, 2 * total), (4, block, total)),
        name="transform",
    )(*pays, own, screen, staged)
    arrived = spread_along(weighted, ri)
    part = pl.pallas_call(
        lambda *refs: contract_kernel(ri, ao, block, *refs),
        out_shape=jax.ShapeDtypeStruct((ri_rows, 2 * ri), jnp.float32),
        in_specs=[vmem] * (len(arrived) + 1),
        out_specs=vmem,
        compiler_params=room((half * len(arrived), block), (2 * ri_rows, block, total)),
        name="contract",
    )(*arrived, staged)
    parts = [part] + [exchange(part, "ao", ao, k) for k in range(1, ao)]
    while len(parts) > 1:
        parts = [parts[i] + parts[i + 1] for i in range(0, len(parts), 2)]
    return parts[0]


def solution(mesh):
    placed = (P("ri", "ao", None), P("ri", "ao", None), P("ao", None), P("ao", None), P(), P())
    ri, ao = mesh.shape["ri"], mesh.shape["ao"]

    def body(*args):
        return shards(ri, ao, *args)

    return jax.shard_map(body, mesh=mesh, in_specs=placed, out_specs=P("ri", None), check_vma=False)
```

```python
import math

import jax
import jax.numpy as jnp
from jax import lax
from jax.experimental import pallas as pl
from jax.experimental.pallas import tpu as pltpu
from jax.sharding import PartitionSpec as P


ATOM_BS = 16
TILE = 16
TAIL = 8


def top_bit(k):
    return k.bit_length() - 1


def shared(k, ao):
    return ao == 4 and k == 3


def crosses(k, ao):
    return ao == 4 and k in (1, 2)


def which(a, k):
    return lax.shift_right_logical(a, jnp.int32(top_bit(k))) & 1


def tri_masks(block):
    row = lax.broadcasted_iota(jnp.int32, (block, block), 0)
    col = lax.broadcasted_iota(jnp.int32, (block, block), 1)
    return row > col, row == col


def fold_diagonal(first, second, below, on):
    folded = jnp.where(below | on, first, second)
    diagonal = jnp.sum(jnp.where(on, second, 0.0), axis=0, keepdims=True)
    return folded, diagonal


def block_at(ref, index, block):
    return ref[:, pl.ds(pl.multiple_of(index * block, block), block)]


def pieces(shape):
    half = shape[-2] // 2
    halves = [pl.ds(0, half), pl.ds(half, half)]
    return halves if len(shape) == 2 else [(i, x) for i in range(shape[0]) for x in halves]


def prep_kernel(*refs):
    hbm, mask_ref, pay_refs, copied, sems = refs[:5], refs[5], refs[6:-6], refs[-6:-1], refs[-1]
    copies = []
    for i, (src, dst) in enumerate(zip(hbm, copied)):
        parts = [(src, dst)] if i < 2 else [(src.at[x], dst.at[x]) for x in pieces(src.shape)]
        copies += [pltpu.make_async_copy(x, y, sems.at[len(copies) + n]) for n, (x, y) in enumerate(parts)]
    for copy in copies:
        copy.start()
    sizes_ref, pattern_ref, slab_ref, occ_ref, virt_ref = copied
    block = occ_ref.shape[0]
    total = occ_ref.shape[1]
    ao = total // block
    atoms = pattern_ref.shape[0]
    f32, bf16 = jnp.float32, jnp.bfloat16
    a = lax.axis_index("ao")
    row_atom = lax.shift_right_logical(
        lax.broadcasted_iota(jnp.int32, (block, atoms), 0), jnp.int32(4)
    ) + a * (block // ATOM_BS)
    pick_row = row_atom == lax.broadcasted_iota(jnp.int32, (block, atoms), 1)
    col_atom = lax.shift_right_logical(
        lax.broadcasted_iota(jnp.int32, (atoms, total), 1), jnp.int32(4)
    )
    pick_col = (col_atom == lax.broadcasted_iota(jnp.int32, (atoms, total), 0)).astype(f32).astype(bf16)
    copies[0].wait()
    copies[1].wait()
    sizes = sizes_ref[...].astype(f32)
    size_row = jnp.sum(jnp.where(pick_row, jnp.broadcast_to(sizes, (block, atoms)), 0.0), axis=1, keepdims=True)
    size_col = jnp.dot(
        jnp.broadcast_to(sizes, (8, atoms)).astype(bf16), pick_col, preferred_element_type=f32
    )[0:1]
    rows = jnp.dot(
        pick_row.astype(f32).astype(bf16), pattern_ref[...].astype(f32).astype(bf16),
        preferred_element_type=f32,
    ).astype(bf16)
    kept = jnp.dot(rows, pick_col, preferred_element_type=f32)
    slot_row = (lax.broadcasted_iota(jnp.int32, (block, total), 0) & (ATOM_BS - 1)).astype(f32)
    slot_col = (lax.broadcasted_iota(jnp.int32, (block, total), 1) & (ATOM_BS - 1)).astype(f32)
    live = (slot_row < size_row) & (slot_col < size_col)
    mask_ref[...] = jnp.where(live, kept, 0.0).astype(bf16)
    below, on = tri_masks(block)
    for copy in copies[2:]:
        copy.wait()
    even = (lax.axis_index("ri") & 1) == 0
    rows, size = block // 2, (ao - 1) * block

    def put(place, k, whole):
        for m in range(1, ao):
            if m == k or crosses(m, ao) and crosses(k, ao):
                continue
            value, step = whole, block
            if place == 1 and shared(m, ao):
                value, step = jnp.where(even, whole[:rows], whole[rows:]), rows
            at = place * size + ((ao - 2) if k == 0 else k - 1 - (k > m)) * step
            pay_refs[m - 1][at : at + step, :] = value

    tails, held = [], {}
    for k in range(1, ao + 1):
        k %= ao
        screen = block_at(mask_ref, a ^ k, block)
        cols = pl.ds(pl.multiple_of((a ^ k) * block, block), block)
        for place in range(2):
            if place == 0:
                pair = [slab_ref[q, :, cols] * screen for q in range(2)]
            else:
                pair = [occ_ref[:, cols], virt_ref[:, cols]]
            if k:
                value = jnp.where(which(a, k) == 0, *pair)
            else:
                value, diagonal = fold_diagonal(*(x.astype(f32) for x in pair), below, on)
                value = value.astype(bf16)
                tails.append(diagonal)
            put(place, k, value)
            if crosses(k, ao):
                held[place, k] = value
    if held:
        for place in range(2):
            one, two = held[place, 1], held[place, 2]
            pay_refs[0][place * size : place * size + block, :] = jnp.where(even, two, one)
            pay_refs[1][place * size : place * size + block, :] = jnp.where(even, one, two)
    upper = lax.broadcasted_iota(jnp.int32, (2 * TAIL, block), 0) < TAIL
    tail = jnp.where(upper, *tails).astype(bf16)
    for ref in pay_refs:
        ref[ref.shape[0] - 2 * TAIL :, :] = tail


def reader(ref, base, m, ao, block):
    def read(k):
        at = base + ((ao - 2) if k == 0 else k - 1 - (k > m)) * block
        return ref[at : at + block, :]

    return read


def either(chosen, first, second):
    return lambda k: jnp.where(chosen, first(k), second(k))


def halves_reader(mine, other, even, base, m, ao, block):
    here, there = (reader(x, base, m, ao, block // 2) for x in (mine, other))

    def read(k):
        x, y = here(k), there(k)
        return jnp.concatenate([jnp.where(even, x, y), jnp.where(even, y, x)], axis=0)

    return read


def unfold(reads, diagonals, own, a, ao, block, put):
    below, on = tri_masks(block)
    for q in range(2):
        for k in range(ao):
            value = own(q, k)
            put(q, 0, k, value)
            if k:
                put(q, k, 0, value.T)
    for m in range(1, ao):
        for k in range(1, ao):
            if k != m:
                value = reads[m](k)
                put(which(a ^ m, k), m, m ^ k, value)
                put(which(a ^ m, k), m ^ k, m, value.T)
        folded = reads[m](0).astype(jnp.float32)
        folded_t = folded.T
        diagonal = diagonals[m]
        put(0, m, m, jnp.where(below | on, folded, folded_t).astype(jnp.bfloat16))
        put(
            1, m, m,
            jnp.where(below, folded_t, jnp.where(on, jnp.broadcast_to(diagonal, (block, block)), folded)).astype(
                jnp.bfloat16
            ),
        )


def transform_kernel(ao, block, *refs):
    own_ref, screen_ref, _, out_ref, slab_ref, green_ref, left_ref = refs[-7:]
    pays = refs[:-7]
    total = ao * block
    a = lax.axis_index("ao")
    f32, bf16 = jnp.float32, jnp.bfloat16
    size = (ao - 1) * block
    pays, others = pays[: ao - 1], list(pays[ao - 1 :])
    even = (lax.axis_index("ri") & 1) == 0
    slabs, greens, diagonals = [None], [None], ([None], [None])
    for m, x in enumerate(pays, 1):
        tail = x[x.shape[0] - 2 * TAIL :, :].astype(f32)
        if crosses(m, ao):
            other = pays[2 - m]
            tail = jnp.where(even, tail, other[other.shape[0] - 2 * TAIL :, :].astype(f32))
            reads = [
                either(even, reader(x, base, m, ao, block), reader(other, base, m, ao, block)) for base in (0, size)
            ]
        elif shared(m, ao):
            reads = [
                reader(x, 0, m, ao, block), halves_reader(x, others.pop(0), even, size, m, ao, block)
            ]
        else:
            reads = [reader(x, base, m, ao, block) for base in (0, size)]
        slabs.append(reads[0])
        greens.append(reads[1])
        for rows, at in zip(diagonals, (0, TAIL)):
            rows.append(tail[at : at + 1])

    def put_slab(matrix, row, col, value):
        slab_ref[matrix, row * block : (row + 1) * block, col * block : (col + 1) * block] = value

    def put_green(matrix, row, col, value):
        at = pl.multiple_of((1 - matrix) * total + col * block, block)
        green_ref[row, :, pl.ds(at, block)] = value

    def own(first):
        return lambda q, k: own_ref[first + q, :, k * block : (k + 1) * block]

    unfold(slabs, diagonals[0], own(0), a, ao, block, put_slab)
    both = own_ref[2:4].reshape(2 * block, total)
    for q in range(2):
        left = jnp.dot(both, slab_ref[q], preferred_element_type=f32).astype(bf16)
        left_ref[q, :, :total] = left[:block]
        left_ref[q, :, total:] = left[block:]
    unfold(greens, diagonals[1], own(2), a, ao, block, put_green)
    last = (((1,), (1,)), ((), ()))
    below, on = tri_masks(block)

    def put_block(k, sums):
        screen = screen_ref[:, k * block : (k + 1) * block].astype(f32)
        out_ref[(k - 1) * block : k * block, :] = (sums * screen).astype(bf16)

    lefts = jnp.concatenate([left_ref[0], left_ref[1]], axis=0)
    rights = green_ref[0 : min(2, ao)].reshape(min(2, ao) * block, 2 * total)
    sums = lax.dot_general(lefts, rights, last, preferred_element_type=f32)
    weight = jnp.where(on, 0.5, 1.0) * screen_ref[:, 0:block].astype(f32)
    folded, diagonal = fold_diagonal(sums[:block, :block] * weight, sums[block:, :block] * weight, below, on)
    if ao > 1:
        put_block(1, jnp.where(which(a, 1) == 0, sums[:block, block:], sums[block:, block:]))
    start = 2
    while start < ao:
        rights = green_ref[start : 2 * start].reshape(start * block, 2 * total)
        sums = lax.dot_general(left_ref[which(a, start)], rights, last, preferred_element_type=f32)
        for k in range(start, 2 * start):
            put_block(k, sums[:, (k - start) * block : (k - start + 1) * block])
        start *= 2
    at = (ao - 1) * block
    out_ref[at : at + block, :] = folded.astype(bf16)
    out_ref[at + block :, :] = jnp.broadcast_to(diagonal, (TAIL, block)).astype(bf16)


def stage_kernel(tensor_hbm, slab_hbm, occ_hbm, virt_hbm, mask_ref, out_ref, own_ref, screen_ref, *scratch):
    tensor_ref, slab_ref, occ_ref, virt_ref, rows_ref, sems = scratch
    ri_rows, block, _ = tensor_ref.shape
    a = lax.axis_index("ao")
    sources = (slab_hbm, occ_hbm, virt_hbm, tensor_hbm)
    targets = (slab_ref, occ_ref, virt_ref, tensor_ref)
    copies = [pltpu.make_async_copy(x, y, sems.at[i]) for i, (x, y) in enumerate(zip(sources, targets))]
    for copy in copies:
        copy.start()
    for copy in copies[:3]:
        copy.wait()
    for k in range(out_ref.shape[0]):
        cols = pl.ds(pl.multiple_of((a ^ k) * block, block), block)
        span = slice(k * block, (k + 1) * block)
        screen = mask_ref[:, cols]
        screen_ref[:, span] = screen
        for q in range(2):
            own_ref[q, :, span] = slab_ref[q, :, cols] * screen
        own_ref[2, :, span] = occ_ref[:, cols]
        own_ref[3, :, span] = virt_ref[:, cols]
    copies[3].wait()
    for k in range(out_ref.shape[0]):
        cols = pl.ds(pl.multiple_of((a ^ k) * block, block), block)
        for g in range(block // TILE):
            for p in range(ri_rows):
                rows_ref[p * TILE : (p + 1) * TILE, :] = tensor_ref[p, g * TILE : (g + 1) * TILE, cols]
            out_ref[k, g * block : (g + 1) * block, :] = rows_ref[...].T


def contract_kernel(count, ao, block, *refs):
    pays = refs[:count]
    tensor_ref, out_ref = refs[count:]
    ri_rows = tensor_ref.shape[2] // TILE
    a = lax.axis_index("ao")
    r = lax.axis_index("ri")
    f32, bf16 = jnp.float32, jnp.bfloat16
    groups = block // TILE
    last, plain = (((1,), (1,)), ((), ())), (((1,), (0,)), ((), ()))

    def spread(values, rows_of):
        return jnp.concatenate(
            [
                jnp.concatenate([rows_of(v, slice(g * TILE, (g + 1) * TILE)) for v in values], axis=0)
                for g in range(groups)
            ],
            axis=1,
        )

    below, on = tri_masks(block)
    at = (ao - 1) * block
    firsts, seconds = [], []
    for pay in pays:
        folded = pay[at : at + block, :].astype(f32)
        diagonal = pay[at + block : at + block + TAIL, :].astype(f32)[0:1]
        firsts.append(jnp.where(below | on, folded, 0.0).astype(bf16))
        seconds.append(
            jnp.where(below, 0.0, jnp.where(on, jnp.broadcast_to(diagonal, (block, block)), folded)).astype(bf16)
        )
    sums = lax.dot_general(
        spread(firsts + seconds, lambda v, rows: v[rows]), tensor_ref[0], plain, preferred_element_type=f32
    )
    half, width = count * TILE, ri_rows * TILE
    row = lax.broadcasted_iota(jnp.int32, (half, width), 0)
    col = lax.broadcasted_iota(jnp.int32, (half, width), 1)
    same = (row & (TILE - 1)) == (col & (TILE - 1))

    def trace(values):
        return jnp.where(same, values, 0.0).reshape(count, TILE, width).sum(axis=1)

    traces = [trace(sums[:half]), trace(sums[half:])]
    first = max(1, ao // 2)
    while first >= 1 and ao > 1:
        lefts = [
            spread(pays, lambda pay, rows, at=(k - 1) * block: pay[at + rows.start : at + rows.stop, :])
            for k in range(first, 2 * first)
        ]
        rights = tensor_ref[first : 2 * first].reshape(first * groups * block, width)
        part = trace(
            lax.dot_general(jnp.concatenate(lefts, axis=1), rights, plain, preferred_element_type=f32)
        )
        to_first = which(a, first) == 0
        traces[0] = traces[0] + jnp.where(to_first, part, 0.0)
        traces[1] = traces[1] + jnp.where(to_first, 0.0, part)
        first //= 2
    traces = jnp.concatenate(traces, axis=0)

    def parts(values):
        out, rest = [], values
        for _ in range(3):
            out.append(rest.astype(bf16))
            rest = rest - out[-1].astype(f32)
        return jnp.concatenate(out, axis=0)

    wide = 3 * 2 * count
    target = lax.broadcasted_iota(jnp.int32, (2 * count, wide), 0)
    source = lax.broadcasted_iota(jnp.int32, (2 * count, wide), 1)
    source = jnp.where(source >= 4 * count, source - 4 * count, source)
    source = jnp.where(source >= 2 * count, source - 2 * count, source)
    second = source >= count
    place = ((jnp.where(second, source - count, source) ^ r) * 2 + second.astype(jnp.int32)) == target
    placed = jnp.dot(place.astype(f32).astype(bf16), parts(traces), preferred_element_type=f32)
    pick = (
        lax.shift_right_logical(lax.broadcasted_iota(jnp.int32, (ri_rows, width), 1), jnp.int32(4))
        == lax.broadcasted_iota(jnp.int32, (ri_rows, width), 0)
    ).astype(f32).astype(bf16)
    split = parts(placed)
    ordered = sum(
        lax.dot_general(
            pick, split[n * 2 * count : (n + 1) * 2 * count], last, preferred_element_type=f32
        )
        for n in range(3)
    )
    out_ref[...] = ordered * (1.0 / (ao * block))


def room(*arrays):
    total = sum(2 * math.prod(shape) for shape in arrays)
    return pltpu.CompilerParams(vmem_limit_bytes=min(2 * total + (4 << 20), 60 << 20))


def exchange(value, axis, size, k):
    return lax.ppermute(value, axis, [(i, i ^ k) for i in range(size)])


def crossed(value, ri, ao, k, j):
    pairs = [(r * ao + a, r * ao + (a ^ (j if r % 2 else k))) for r in range(ri) for a in range(ao)]
    return lax.ppermute(value, ("ri", "ao"), pairs)


def along(value, targets):
    pairs = []
    for source, target in enumerate(targets):
        for core in range(2):
            other = 2 * source + 1 - core if target == source else 2 * target + core
            pairs.append((2 * source + core, other))
    return lax.ppermute(value, "ri", pairs)


def spread_along(value, ri):
    if ri != 8:
        sources = [value] + [exchange(value, "ri", ri, k) for k in range(2, ri, 2)]
        forwards = [exchange(x, "ri", ri, 1) for x in sources]
        return [x for pair in zip(sources, forwards) for x in pair]
    chip = lax.shift_right_logical(lax.axis_index("ri"), jnp.int32(1))
    inner = (chip == 1) | (chip == 2)
    middle = along(value, (0, 2, 1, 3))
    near = along(value, (1, 0, 3, 2))
    far = along(value, (3, 1, 2, 0))
    relayed, middle = lax.optimization_barrier((jnp.where(inner, middle, value), middle))
    last = along(relayed, (2, 0, 3, 1))
    across, other = jnp.where(inner, middle, far), jnp.where(inner, far, middle)
    return [value, other] + [x for y in (near, last, across) for x in (y, exchange(y, "ri", ri, 1))]


def shards(ri, ao, three_center, slab_tensor, occ_green, virt_green, pattern, atom_sizes):
    block = occ_green.shape[0]
    total = occ_green.shape[1]
    ri_rows = three_center.shape[0]
    atoms = pattern.shape[0]
    half = total + TAIL
    bf16 = jnp.bfloat16
    vmem = pl.BlockSpec(memory_space=pltpu.VMEM)
    inputs = tuple(
        pltpu.with_memory_space_constraint(x, pltpu.HBM)
        for x in (atom_sizes.reshape(1, atoms), pattern, slab_tensor, occ_green, virt_green)
    )
    size = (ao - 1) * block
    sizes = [size + (size // 2 if shared(k, ao) else size) + 2 * TAIL for k in range(1, ao)]
    prepared = pl.pallas_call(
        prep_kernel,
        out_shape=[jax.ShapeDtypeStruct((block, total), bf16)]
        + [jax.ShapeDtypeStruct((rows, block), bf16) for rows in sizes],
        in_specs=[pl.BlockSpec(memory_space=pltpu.HBM)] * 5,
        out_specs=[vmem] * (1 + len(sizes)),
        scratch_shapes=[pltpu.VMEM(x.shape, x.dtype) for x in inputs]
        + [pltpu.SemaphoreType.DMA((2 + sum(len(pieces(x.shape)) for x in inputs[2:]),))],
        compiler_params=room((sum(sizes), block), (5 * block, total), (2 * block, 2 * total)),
        name="prep",
    )(*inputs)
    mask, *pays = prepared
    arrived = []
    for k, pay in enumerate(pays, 1):
        arrived.append(crossed(pay, ri, ao, k, 3 - k) if crosses(k, ao) else exchange(pay, "ao", ao, k))
    pays = arrived + [exchange(x, "ri", ri, 1) for k, x in enumerate(arrived, 1) if shared(k, ao)]
    groups = block // TILE
    rows = ri_rows * TILE
    staged, own, screen = pl.pallas_call(
        stage_kernel,
        out_shape=[
            jax.ShapeDtypeStruct((ao, groups * block, rows), bf16),
            jax.ShapeDtypeStruct((4, block, total), bf16),
            jax.ShapeDtypeStruct((block, total), bf16),
        ],
        in_specs=[pl.BlockSpec(memory_space=pltpu.HBM)] * 4 + [vmem],
        out_specs=[vmem] * 3,
        scratch_shapes=[pltpu.VMEM(x.shape, bf16) for x in (three_center, *inputs[2:])]
        + [pltpu.VMEM((rows, block), bf16), pltpu.SemaphoreType.DMA((4,))],
        compiler_params=room((2 * ri_rows, block, total), (8 * block, total)),
        cost_estimate=pl.CostEstimate(flops=0, transcendentals=0, bytes_accessed=8 * ri_rows * block * total),
        name="stage",
    )(pltpu.with_memory_space_constraint(three_center, pltpu.HBM), *inputs[2:], mask)
    weighted = pl.pallas_call(
        lambda *refs: transform_kernel(ao, block, *refs),
        out_shape=jax.ShapeDtypeStruct((half, block), bf16),
        in_specs=[vmem] * (len(pays) + 2) + [pl.BlockSpec(memory_space=pl.ANY)],
        out_specs=vmem,
        scratch_shapes=[
            pltpu.VMEM((2, total, total), bf16),
            pltpu.VMEM((ao, block, 2 * total), bf16),
            pltpu.VMEM((2, block, 2 * total), bf16),
        ],
        compiler_params=room((sum(sizes), block), (4 * block, total), (2, total, total), (ao, block, 2 * total), (4, block, total)),
        name="transform",
    )(*pays, own, screen, staged)
    arrived = spread_along(weighted, ri)
    part = pl.pallas_call(
        lambda *refs: contract_kernel(ri, ao, block, *refs),
        out_shape=jax.ShapeDtypeStruct((ri_rows, 2 * ri), jnp.float32),
        in_specs=[vmem] * (len(arrived) + 1),
        out_specs=vmem,
        compiler_params=room((half * len(arrived), block), (2 * ri_rows, block, total)),
        name="contract",
    )(*arrived, staged)
    parts = [part] + [exchange(part, "ao", ao, k) for k in range(1, ao)]
    while len(parts) > 1:
        parts = [parts[i] + parts[i + 1] for i in range(0, len(parts), 2)]
    return parts[0]


def solution(mesh):
    placed = (P("ri", "ao", None), P("ri", "ao", None), P("ao", None), P("ao", None), P(), P())
    ri, ao = mesh.shape["ri"], mesh.shape["ao"]

    def body(*args):
        return shards(ri, ao, *args)

    return jax.shard_map(body, mesh=mesh, in_specs=placed, out_specs=P("ri", None), check_vma=False)
```
